32 devices in a mesh: parts: 2 (over y), src: 4 (over x, core), space: 4 (over z).
Axes of the slice: x: 2, y: 2, z: 4, core: 2. Of those that a mesh axis runs over, the one named last changes fastest.
Arguments:
- fields: float32 [8, 4, 16, 128, 128], P(('parts', 'src'), None, 'space'), parts along dimension 0, may hold values from -6 to 6
- velocity: float32 [32, 128, 128], P(('parts', 'space')), parts along dimension 0, may hold values from 0.5 to 1
- conductivity: float32 [32, 128, 128], P(('parts', 'space')), parts along dimension 0, may hold values from 1 to 4
- labels: int32 [8], P(('parts', 'src')), parts along dimension 0, may hold values from 0 to 1, as said below
Outputs:
- fields_out: float32 [8, 2, 16, 128, 128], P(('parts', 'src'), None, 'space'), parts along dimension 0
- models_out: float32 [2, 32, 128, 128], P(None, ('parts', 'space')), parts along dimension 1
The draws below stay inside these ranges and needn't reach their ends.
There are 2 independent parts, one for each index of `parts`. The reference program is written for one: setup_inputs(seed, part) draws one part's arguments, and reference() takes and returns one part's arrays. A program takes and returns all parts, laid end to end along the dimension named above; each array names one. Nothing has to cross between parts.
Inputs may be any that keep to these rules, and one draw needn't show every extreme that they name: `labels`: at least one group has label 0 and at least one has label 1; the rest are drawn.
All inputs are finite; a program needn't handle non-finite values.
Results may differ from the reference program's by a relative error of at most 0.00002.
Values sent between devices are 32-bit elements; how exact they have to be, the bound alone decides.
No kernel may reach another device: no remote copies, remote signals or barrier semaphores. Data moves between devices by JAX's collectives and lax.ppermute only.
A program may use at most 64 MiB of HBM per device.

```python
import math
import jax
import jax.numpy as jnp
from jax import lax

NY = 128
NZ = 128
STEPS = 3
G = 4
NX = 16


def draw_labels(key, part):
    key_bits = jax.random.fold_in(key, 11)
    key_zero = jax.random.fold_in(key, 23)
    key_one = jax.random.fold_in(key, 37)
    bits = jax.random.randint(key_bits, (G,), 0, 2).astype(jnp.int32)
    zero_pos = jax.random.randint(key_zero, (), 0, G).astype(jnp.int32)
    step_one = jax.random.randint(key_one, (), 1, G).astype(jnp.int32)
    one_pos = ((zero_pos + step_one) % G).astype(jnp.int32)
    bits = bits.at[zero_pos].set(0).at[one_pos].set(1)
    return bits.astype(jnp.int32)


def block_levels(stream_key, extent, cuts, smallest, largest):
    factor_of, own = 1.0, jax.random.fold_in(stream_key, 6)
    for dim, parts in cuts:
        draws = jnp.exp(jax.random.uniform(jax.random.fold_in(own, dim), (parts,), jnp.float32, smallest / len(cuts), largest / len(cuts)))
        factor_of = factor_of * jnp.repeat(draws, extent[dim] // parts).reshape([-1 if axis == dim else 1 for axis in range(len(extent))])
    return factor_of


def noise(rng, dims, width, most, split=(), dtype=jnp.bfloat16):
    values = jax.random.normal(rng, dims, jnp.float32) * width
    if len(split) > 0:
        values = block_levels(rng, dims, split, -0.22, 0.18) * values
    return jnp.clip(values, min=-most, max=most).astype(dtype)


def setup_inputs(seed: int = 0, part: int = 0) -> dict:
    seeds = jax.random.split(jax.random.key(seed), 5)
    own_keys = jax.random.split(jax.random.fold_in(seeds[4], part), 5)
    fields = noise(own_keys[0], (G, 4, NX, NY, NZ), 1.0, 6.0, ((0, 4), (2, 4)), jnp.float32)
    velocity = jnp.clip(0.5 + 0.5 * jax.random.uniform(own_keys[1], (NX, NY, NZ), jnp.float32) ** block_levels(own_keys[1], (NX, NY, NZ), ((0, 4),), -0.2, 0.2), 0.5, 1.0)
    conductivity = jnp.clip(jnp.exp(math.log(4.0) - 1.3862944 * jax.random.uniform(own_keys[2], (NX, NY, NZ), jnp.float32) ** block_levels(own_keys[2], (NX, NY, NZ), ((0, 4),), -0.2, 0.2)), 1.0, 4.0)
    labels = draw_labels(jax.random.fold_in(jax.random.fold_in(seeds[4], part), 71), part)
    return dict(fields=fields, velocity=velocity, conductivity=conductivity, labels=labels)


speed_gain = 0.25
diffuse_gain = 0.15
step_size = 0.1
penalty_gain = 50.0

def laplace(field):
    padded = jnp.pad(field, 1)
    total = padded[2:, 1:-1, 1:-1] + padded[:-2, 1:-1, 1:-1]
    total = total + padded[1:-1, 2:, 1:-1] + padded[1:-1, :-2, 1:-1]
    total = total + padded[1:-1, 1:-1, 2:] + padded[1:-1, 1:-1, :-2]
    return total - 6.0 * field

def coefficient(weight, velocity, conductivity):
    return weight * speed_gain * velocity ** 2 + (1.0 - weight) * diffuse_gain / conductivity

def advance(state, coef, weight):
    upper, upper_prev, lower, lower_prev = state
    accum = jnp.zeros_like(upper)
    for step in range(STEPS):
        lap_upper = laplace(upper)
        lap_lower = laplace(lower)
        accum = accum + lower * lap_upper
        upper_next = weight * (2.0 * upper - upper_prev) + (1.0 - weight) * upper + coef * lap_upper
        lower_next = weight * (2.0 * lower - lower_prev) + (1.0 - weight) * lower + coef * lap_lower
        upper_prev, upper = (upper, upper_next)
        lower_prev, lower = (lower, lower_next)
    return ((upper, upper_prev, lower, lower_prev), accum)

def centred(model):
    padded = jnp.pad(model, 1, mode='edge')
    along_x = (padded[2:, 1:-1, 1:-1] - padded[:-2, 1:-1, 1:-1]) * 0.5
    along_y = (padded[1:-1, 2:, 1:-1] - padded[1:-1, :-2, 1:-1]) * 0.5
    along_z = (padded[1:-1, 1:-1, 2:] - padded[1:-1, 1:-1, :-2]) * 0.5
    return (along_x, along_y, along_z)

def reference(fields, velocity, conductivity, labels):
    weights = labels.astype(jnp.float32)

    def first(item):
        group, weight = item
        coef = coefficient(weight, velocity, conductivity)
        state, accum = advance((group[0], group[1], group[2], group[3]), coef, weight)
        return (jnp.stack(state, 0), accum)
    states, accums = lax.map(first, (fields, weights))
    scale = 1.0 / (20.0 * jnp.sqrt(jnp.float32(G)))
    wide = weights[:, None, None, None]
    grad_v = scale * lax.optimization_barrier(jnp.sum(wide * accums, 0))
    grad_c = scale * lax.optimization_barrier(jnp.sum((1.0 - wide) * accums, 0))
    vx, vy, vz = centred(velocity)
    lx, ly, lz = centred(jnp.log(conductivity))
    cross_a = vy * lz - vz * ly
    cross_b = vz * lx - vx * lz
    cross_c = vx * ly - vy * lx
    penalty = penalty_gain * (cross_a * cross_a + cross_b * cross_b + cross_c * cross_c)
    new_velocity = velocity * jnp.exp(-step_size * jnp.tanh(grad_v + penalty))
    new_conductivity = conductivity * jnp.exp(-step_size * jnp.tanh(grad_c + penalty))

    def second(item):
        state, weight = item
        coef = coefficient(weight, new_velocity, new_conductivity)
        final, unused = advance((state[0], state[1], state[2], state[3]), coef, weight)
        return jnp.stack([final[0], final[2]], 0)
    fields_out = lax.map(second, (states, weights))
    return (fields_out, jnp.stack([new_velocity, new_conductivity], 0))
```

```python
import math

import jax
import jax.numpy as jnp
from jax import lax
from jax.experimental import pallas as pl
from jax.experimental.pallas import tpu as pltpu
from jax.sharding import PartitionSpec as P

speed_gain = 0.25
diffuse_gain = 0.15
step_size = 0.1
penalty_gain = 50.0

VMEM = pl.BlockSpec(memory_space=pltpu.VMEM)
SMEM = pl.BlockSpec(memory_space=pltpu.SMEM)
F32 = jnp.float32


def call(kernel, outs, args, specs, name, scratch=()):
    size = sum(math.prod(o) for o in outs) + sum(a.size for a in args)
    return pl.pallas_call(
        kernel,
        out_shape=tuple(jax.ShapeDtypeStruct(o, F32) for o in outs),
        in_specs=specs,
        out_specs=tuple(VMEM for _ in outs),
        scratch_shapes=list(scratch),
        name=name,
        cost_estimate=pl.CostEstimate(flops=20 * size, bytes_accessed=4 * size, transcendentals=0),
    )(*args)


def plane_tools(shape):
    row = lax.broadcasted_iota(jnp.int32, shape, 0)
    col = lax.broadcasted_iota(jnp.int32, shape, 1)
    rows, cols = shape

    def shifts(p, edge):
        def fill(test, moved):
            return jnp.where(test, p if edge else 0.0, moved)

        return (
            fill(row == 0, pltpu.roll(p, 1, 0)),
            fill(row == rows - 1, pltpu.roll(p, rows - 1, 0)),
            fill(col == 0, pltpu.roll(p, 1, 1)),
            fill(col == cols - 1, pltpu.roll(p, cols - 1, 1)),
        )

    def flat(p):
        a, b, c, d = shifts(p, False)
        return ((a + b) + (c + d)) - 6.0 * p

    return shifts, flat


def coefficient(weight, velocity, conductivity):
    return weight * speed_gain * velocity**2 + (1.0 - weight) * diffuse_gain / conductivity


def isolated_kernel(meta, f_ref, v_ref, c_ref, e_ref, o_ref, coef_ref, s1, s2):
    a = meta[0].astype(F32)
    even = meta[1] == 0
    tile = f_ref.shape[2]
    _, flat = plane_tools(f_ref.shape[3:])
    for i in range(tile):
        coef_ref[i] = coefficient(a, v_ref[i], c_ref[i])

    def lap(ref, i):
        total = flat(ref[i])
        if i > 0:
            total = total + ref[i - 1]
        if i < tile - 1:
            total = total + ref[i + 1]
        return total

    for n in range(2):
        cur, prev = f_ref.at[0, 2 * n], f_ref.at[0, 2 * n + 1]
        for i in range(tile):
            s1[i] = (1.0 + a) * cur[i] - a * prev[i] + coef_ref[i] * lap(cur, i)
        for i in (0, tile - 1):
            s2[i] = (1.0 + a) * s1[i] - a * cur[i] + coef_ref[i] * lap(s1, i)
        for k, ref in enumerate((s1, s2)):
            low, high = ref[0], ref[tile - 1]
            e_ref[2 * n + k] = jnp.where(even, high, low)
            o_ref[2 * n + k] = jnp.where(even, low, high)


def sides(even, e_ref, o_ref, k):
    e, o = e_ref[k], o_ref[k]
    return jnp.where(even, o, e), jnp.where(even, e, o)


def model_halo(meta, pick):
    first = meta[4] == 0
    out = []
    for s in range(2):
        mine, other = pick[0][s], pick[1][s]
        has = meta[2 + s] == 1
        out.append(
            (
                jnp.where(has, jnp.where(first, mine, other), 1.0),
                jnp.where(has, jnp.where(first, other, mine), 1.0),
                has,
            )
        )
    return out


def first_kernel(
    meta, f_ref, coef_ref, e1, o1, m_e, m_o, e2, o2,
    acc_ref, st_ref, hb_ref, hc_ref, pe_ref, po_ref, one,
):
    a = meta[0].astype(F32)
    even = meta[1] == 0
    tile, ny = f_ref.shape[2], f_ref.shape[3]
    _, flat = plane_tools(f_ref.shape[3:])
    edge = (0, tile - 1)
    halo = model_halo(meta, (sides(even, e1, o1, 0), sides(even, m_e, m_o, 0)))
    for s in range(2):
        v, c, has = halo[s]
        hc_ref[s] = jnp.where(has, coefficient(a, v, c), 0.0)

    def lap(ref, i, h):
        below = ref[i - 1] if i > 0 else h[0]
        above = ref[i + 1] if i < tile - 1 else h[1]
        return flat(ref[i]) + (below + above)

    for n in (1, 0):
        cur, prev = f_ref.at[0, 2 * n], f_ref.at[0, 2 * n + 1]
        two, three = st_ref.at[n, 0], st_ref.at[n, 1]
        h0 = sides(even, e1, o1, 1 + n)
        h1 = sides(even, e2, o2, 2 * n)
        h2 = sides(even, e2, o2, 2 * n + 1)
        d = [hc_ref[s] * cur[edge[s]] for s in range(2)]
        h1 = [h1[s] + d[s] for s in range(2)]
        for i in range(tile):
            l = lap(cur, i, h0)
            if n == 0:
                acc_ref[i * ny:(i + 1) * ny] = f_ref[0, 2, i] * l
            one[n, i] = (1.0 + a) * cur[i] - a * prev[i] + coef_ref[i] * l
        h2 = [
            h2[s] + (1.0 + a) * d[s] + hc_ref[s] * (flat(d[s]) + one[n, edge[s]])
            for s in range(2)
        ]
        for i in range(tile):
            l = lap(one.at[n], i, h1)
            if n == 0:
                acc_ref[i * ny:(i + 1) * ny] += one[1, i] * l
            two[i] = (1.0 + a) * one[n, i] - a * cur[i] + coef_ref[i] * l
        for i in range(tile):
            l = lap(two, i, h2)
            if n == 0:
                acc_ref[i * ny:(i + 1) * ny] += st_ref[1, 0, i] * l
            three[i] = (1.0 + a) * two[i] - a * one[n, i] + coef_ref[i] * l
        for s in range(2):
            hb_ref[s, n, 0] = h2[s]
            hb_ref[s, n, 1] = (
                (1.0 + a) * h2[s] - a * h1[s] + hc_ref[s] * (flat(h2[s]) + two[edge[s]])
            )
        low = (two[1], three[1], three[2])
        high = (two[tile - 2], three[tile - 2], three[tile - 3])
        for k in range(3):
            pe_ref[3 * n + k] = jnp.where(even, high[k], low[k])
            po_ref[3 * n + k] = jnp.where(even, low[k], high[k])
    acc_ref[tile * ny:] = jnp.full((acc_ref.shape[0] - tile * ny, acc_ref.shape[1]), a, F32)


def penalty_kernel(meta, v_ref, c_ref, e1, o1, m_e, m_o, out_ref, logs):
    even = meta[1] == 0
    tile = v_ref.shape[0]
    shifts, _ = plane_tools(v_ref.shape[1:])
    halo = model_halo(meta, (sides(even, e1, o1, 0), sides(even, m_e, m_o, 0)))
    for i in range(tile):
        logs[i + 1] = jnp.log(c_ref[i])
    for s, at, own in ((0, 0, 1), (1, tile + 1, tile)):
        logs[at] = jnp.where(halo[s][2], jnp.log(halo[s][1]), logs[own])
    ends = (
        jnp.where(halo[0][2], halo[0][0], v_ref[0]),
        jnp.where(halo[1][2], halo[1][0], v_ref[tile - 1]),
    )
    for i in range(tile):
        below = v_ref[i - 1] if i > 0 else ends[0]
        above = v_ref[i + 1] if i < tile - 1 else ends[1]
        vx = (above - below) * 0.5
        lx = (logs[i + 2] - logs[i]) * 0.5
        p, q, r, t = shifts(v_ref[i], True)
        vy, vz = (q - p) * 0.5, (t - r) * 0.5
        p, q, r, t = shifts(logs[i + 1], True)
        ly, lz = (q - p) * 0.5, (t - r) * 0.5
        ca = vy * lz - vz * ly
        cb = vz * lx - vx * lz
        cc = vx * ly - vy * lx
        out_ref[i] = penalty_gain * (ca * ca + cb * cb + cc * cc)


def weigh_kernel(mine, other, out_ref):
    tile, ny = out_ref.shape[1:3]
    for ref in (mine, other):
        label = jnp.broadcast_to(ref[tile * ny:tile * ny + 1], out_ref.shape[2:])
        for i in range(tile):
            acc = ref[i * ny:(i + 1) * ny]
            if ref is mine:
                out_ref[0, i] = label * acc
                out_ref[1, i] = (1.0 - label) * acc
            else:
                out_ref[0, i] += label * acc
                out_ref[1, i] += (1.0 - label) * acc


def renew_kernel(scale, meta, p_ref, q_ref, pen_ref, v_ref, c_ref, m_ref, coef_ref, e_ref, o_ref):
    a = meta[0].astype(F32)
    even = meta[1] == 0
    tile = v_ref.shape[0]
    for i in range(tile):
        new = []
        for n, ref in enumerate((v_ref, c_ref)):
            grad = scale * (p_ref[n, i] + q_ref[n, i])
            new.append(ref[i] * jnp.exp(-step_size * jnp.tanh(grad + pen_ref[i])))
            m_ref[n, i] = new[n]
        coef_ref[i] = coefficient(a, *new)
    for k in range(2):
        low, high = coef_ref[k], coef_ref[tile - 2 + k]
        e_ref[k] = jnp.where(even, high, low)
        o_ref[k] = jnp.where(even, low, high)


def second_kernel(meta, st_ref, hb_ref, hc_ref, re, ro, coef_ref, ce, co, out_ref, s3, s4, s5):
    a = meta[0].astype(F32)
    even = meta[1] == 0
    tile = st_ref.shape[2]
    _, flat = plane_tools(st_ref.shape[3:])
    far, near = sides(even, ce, co, 0), sides(even, ce, co, 1)
    cn = {-2: far[0], -1: near[0], tile: far[1], tile + 1: near[1]}

    def coef(j):
        return coef_ref[j] if 0 <= j < tile else cn[j]

    def lap(ref, j, off):
        return flat(ref[j + off]) + (ref[j + off - 1] + ref[j + off + 1])

    for n in range(2):
        two = sides(even, re, ro, 3 * n)
        s3[2], s3[tile + 3] = (hb_ref[s, n, 1] + hc_ref[s] * two[s] for s in range(2))
        s3[1], s3[tile + 4] = sides(even, re, ro, 3 * n + 1)
        s3[0], s3[tile + 5] = sides(even, re, ro, 3 * n + 2)
        prev = {-2: two[0], -1: hb_ref[0, n, 0], tile: hb_ref[1, n, 0], tile + 1: two[1]}
        for i in range(tile):
            s3[i + 3] = st_ref[n, 1, i]
        for j in range(-2, tile + 2):
            before = st_ref[n, 0, j] if 0 <= j < tile else prev[j]
            s4[j + 2] = (1.0 + a) * s3[j + 3] - a * before + coef(j) * lap(s3, j, 3)
        for j in range(-1, tile + 1):
            s5[j + 1] = (1.0 + a) * s4[j + 2] - a * s3[j + 3] + coef(j) * lap(s4, j, 2)
        for j in range(tile):
            out_ref[0, n, j] = (1.0 + a) * s5[j + 1] - a * s4[j + 2] + coef(j) * lap(s5, j, 1)


def swap_pairs(even_block, odd_block):
    count = lax.axis_size("space")
    evens = [(i, i ^ 1) for i in range(count) if i ^ 1 < count]
    odds = [(i, ((i + 1) ^ 1) - 1) for i in range(count) if 0 <= ((i + 1) ^ 1) - 1 < count]
    return lax.ppermute(even_block, "space", evens), lax.ppermute(odd_block, "space", odds)


def across(block, mask):
    count = lax.axis_size("src")
    return lax.ppermute(block, "src", [(i, i ^ mask) for i in range(count)])


def shards(fields, velocity, conductivity, labels):
    tile, ny, nz = velocity.shape
    plane = (ny, nz)
    here, count = lax.axis_index("space"), lax.axis_size("space")
    core = lax.axis_index("src") % 2
    meta = jnp.stack(
        [
            labels[0],
            here % 2,
            (here > 0).astype(jnp.int32),
            (here < count - 1).astype(jnp.int32),
            core,
        ]
    )
    even = here % 2 == 0

    edges = []
    for at in (0, tile - 1):
        model = jnp.where(core == 0, velocity[at], conductivity[at])
        edges.append(jnp.stack([model, fields[0, 0, at], fields[0, 2, at]], 0))
    low, high = edges
    e1, o1 = swap_pairs(jnp.where(even, high, low), jnp.where(even, low, high))

    stack = pltpu.VMEM((tile, *plane), F32)
    e2, o2, coef = call(
        isolated_kernel,
        [(4, *plane), (4, *plane), (tile, *plane)],
        (meta, fields, velocity, conductivity),
        [SMEM, VMEM, VMEM, VMEM],
        "isolated",
        [stack, stack],
    )
    e2, o2 = swap_pairs(e2, o2)
    other = across(jnp.stack([e1[:1], o1[:1]]), 1)
    m_e, m_o = other[0], other[1]

    acc, state, halo, halo_coef, e3, o3 = call(
        first_kernel,
        [
            (tile * ny + 8, nz),
            (2, 2, tile, *plane),
            (2, 2, 2, *plane),
            (2, *plane),
            (6, *plane),
            (6, *plane),
        ],
        (meta, fields, coef, e1, o1, m_e, m_o, e2, o2),
        [SMEM] + [VMEM] * 8,
        "first",
        [pltpu.VMEM((2, tile, *plane), F32)],
    )

    groups = lax.axis_size("src")
    masks = [1 << k for k in reversed(range(groups.bit_length() - 1))]
    acc_other = across(acc, masks[0])
    e3, o3 = swap_pairs(e3, o3)
    (pen,) = call(
        penalty_kernel,
        [(tile, *plane)],
        (meta, velocity, conductivity, e1, o1, m_e, m_o),
        [SMEM] + [VMEM] * 6,
        "penalty",
        [pltpu.VMEM((tile + 2, *plane), F32)],
    )
    (part,) = call(weigh_kernel, [(2, tile, *plane)], (acc, acc_other), [VMEM] * 2, "weigh")
    for mask in masks[1:-1]:
        part = part + across(part, mask)
    rest = across(part, masks[-1])

    scale = 1.0 / (20.0 * math.sqrt(groups * labels.shape[0]))
    models, coef_next, e4, o4 = call(
        lambda *refs: renew_kernel(scale, *refs),
        [(2, tile, *plane), (tile, *plane), (2, *plane), (2, *plane)],
        (meta, part, rest, pen, velocity, conductivity),
        [SMEM] + [VMEM] * 5,
        "renew",
    )
    e4, o4 = swap_pairs(e4, o4)
    (final,) = call(
        second_kernel,
        [(1, 2, tile, *plane)],
        (meta, state, halo, halo_coef, e3, o3, coef_next, e4, o4),
        [SMEM] + [VMEM] * 8,
        "second",
        [
            pltpu.VMEM((tile + 6, *plane), F32),
            pltpu.VMEM((tile + 4, *plane), F32),
            pltpu.VMEM((tile + 2, *plane), F32),
        ],
    )
    return final, models


def solution(mesh):
    in_specs = (
        P(("parts", "src"), None, "space", None, None),
        P(("parts", "space"), None, None),
        P(("parts", "space"), None, None),
        P(("parts", "src")),
    )
    out_specs = (
        P(("parts", "src"), None, "space", None, None),
        P(None, ("parts", "space"), None, None),
    )
    return jax.shard_map(shards, mesh=mesh, in_specs=in_specs, out_specs=out_specs, check_vma=False)
```

```python
import math

import jax
import jax.numpy as jnp
from jax import lax
from jax.experimental import pallas as pl
from jax.experimental.pallas import tpu as pltpu
from jax.sharding import PartitionSpec as P


speed_gain = 0.25
diffuse_gain = 0.15
step_size = 0.1
penalty_gain = 50.0

VMEM = pl.BlockSpec(memory_space=pltpu.VMEM)
SMEM = pl.BlockSpec(memory_space=pltpu.SMEM)
F32 = jnp.float32


def call(kernel, outs, args, specs, scratch=()):
    size = sum(math.prod(o) for o in outs) + sum(a.size for a in args)
    return pl.pallas_call(
        kernel,
        out_shape=tuple(jax.ShapeDtypeStruct(o, F32) for o in outs),
        in_specs=specs,
        out_specs=tuple(VMEM for _ in outs),
        scratch_shapes=list(scratch),
        compiler_params=pltpu.CompilerParams(vmem_limit_bytes=16 << 20),
        cost_estimate=pl.CostEstimate(flops=20 * size, bytes_accessed=4 * size, transcendentals=0),
    )(*args)


def plane_tools(shape):
    row = lax.broadcasted_iota(jnp.int32, shape, 0)
    col = lax.broadcasted_iota(jnp.int32, shape, 1)
    rows, cols = shape

    def shifts(p, edge):
        def fill(test, moved):
            return jnp.where(test, p if edge else 0.0, moved)

        return (
            fill(row == 0, pltpu.roll(p, 1, 0)),
            fill(row == rows - 1, pltpu.roll(p, rows - 1, 0)),
            fill(col == 0, pltpu.roll(p, 1, 1)),
            fill(col == cols - 1, pltpu.roll(p, cols - 1, 1)),
        )

    def flat(p):
        a, b, c, d = shifts(p, False)
        return ((a + b) + (c + d)) - 6.0 * p

    return shifts, flat


def coefficient(weight, velocity, conductivity):
    return weight * speed_gain * velocity**2 + (1.0 - weight) * diffuse_gain / conductivity


def isolated_kernel(meta, f_ref, v_ref, c_ref, e_ref, o_ref, coef_ref, s1, s2):
    a = meta[0].astype(F32)
    even = meta[1] == 0
    tile = f_ref.shape[2]
    _, flat = plane_tools(f_ref.shape[3:])
    for i in range(tile):
        coef_ref[i] = coefficient(a, v_ref[i], c_ref[i])

    def lap(ref, i):
        total = flat(ref[i])
        if i > 0:
            total = total + ref[i - 1]
        if i < tile - 1:
            total = total + ref[i + 1]
        return total

    for n in range(2):
        cur, prev = f_ref.at[0, 2 * n], f_ref.at[0, 2 * n + 1]
        for i in range(tile):
            s1[i] = (1.0 + a) * cur[i] - a * prev[i] + coef_ref[i] * lap(cur, i)
        for i in (0, tile - 1):
            s2[i] = (1.0 + a) * s1[i] - a * cur[i] + coef_ref[i] * lap(s1, i)
        for k, ref in enumerate((s1, s2)):
            low, high = ref[0], ref[tile - 1]
            e_ref[2 * n + k] = jnp.where(even, high, low)
            o_ref[2 * n + k] = jnp.where(even, low, high)


def sides(even, e_ref, o_ref, k):
    e, o = e_ref[k], o_ref[k]
    return jnp.where(even, o, e), jnp.where(even, e, o)


def model_halo(meta, pick):
    first = meta[4] == 0
    out = []
    for s in range(2):
        mine, other = pick[0][s], pick[1][s]
        has = meta[2 + s] == 1
        out.append(
            (
                jnp.where(has, jnp.where(first, mine, other), 1.0),
                jnp.where(has, jnp.where(first, other, mine), 1.0),
                has,
            )
        )
    return out


def pick_kernel(e1, o1, out_ref):
    out_ref[0] = e1[0]
    out_ref[1] = o1[0]


def first_kernel(
    meta, f_ref, coef_ref, e1, o1, m, e2, o2,
    acc_ref, st_ref, hb_ref, hc_ref, pe_ref, po_ref, one,
):
    a = meta[0].astype(F32)
    even = meta[1] == 0
    tile, ny = f_ref.shape[2], f_ref.shape[3]
    _, flat = plane_tools(f_ref.shape[3:])
    edge = (0, tile - 1)
    halo = model_halo(meta, (sides(even, e1, o1, 0), sides(even, m.at[:1], m.at[1:], 0)))
    for s in range(2):
        v, c, has = halo[s]
        hc_ref[s] = jnp.where(has, coefficient(a, v, c), 0.0)

    def lap(ref, i, h):
        below = ref[i - 1] if i > 0 else h[0]
        above = ref[i + 1] if i < tile - 1 else h[1]
        return flat(ref[i]) + (below + above)

    for n in (1, 0):
        cur, prev = f_ref.at[0, 2 * n], f_ref.at[0, 2 * n + 1]
        two, three = st_ref.at[n, 0], st_ref.at[n, 1]
        h0 = sides(even, e1, o1, 1 + n)
        h1 = sides(even, e2, o2, 2 * n)
        h2 = sides(even, e2, o2, 2 * n + 1)
        d = [hc_ref[s] * cur[edge[s]] for s in range(2)]
        h1 = [h1[s] + d[s] for s in range(2)]
        for i in range(tile):
            l = lap(cur, i, h0)
            if n == 0:
                acc_ref[i * ny:(i + 1) * ny] = f_ref[0, 2, i] * l
            one[n, i] = (1.0 + a) * cur[i] - a * prev[i] + coef_ref[i] * l
        h2 = [
            h2[s] + (1.0 + a) * d[s] + hc_ref[s] * (flat(d[s]) + one[n, edge[s]])
            for s in range(2)
        ]
        for i in range(tile):
            l = lap(one.at[n], i, h1)
            if n == 0:
                acc_ref[i * ny:(i + 1) * ny] += one[1, i] * l
            two[i] = (1.0 + a) * one[n, i] - a * cur[i] + coef_ref[i] * l
        for i in range(tile):
            l = lap(two, i, h2)
            if n == 0:
                acc_ref[i * ny:(i + 1) * ny] += st_ref[1, 0, i] * l
            three[i] = (1.0 + a) * two[i] - a * one[n, i] + coef_ref[i] * l
        for s in range(2):
            hb_ref[s, n, 0] = h2[s]
            hb_ref[s, n, 1] = (
                (1.0 + a) * h2[s] - a * h1[s] + hc_ref[s] * (flat(h2[s]) + two[edge[s]])
            )
        low = (two[1], three[1], three[2])
        high = (two[tile - 2], three[tile - 2], three[tile - 3])
        for k in range(3):
            pe_ref[3 * n + k] = jnp.where(even, high[k], low[k])
            po_ref[3 * n + k] = jnp.where(even, low[k], high[k])
    acc_ref[tile * ny:] = jnp.full((acc_ref.shape[0] - tile * ny, acc_ref.shape[1]), a, F32)


def penalty_kernel(meta, v_ref, c_ref, e1, o1, m, out_ref, logs):
    even = meta[1] == 0
    tile = v_ref.shape[0]
    shifts, _ = plane_tools(v_ref.shape[1:])
    halo = model_halo(meta, (sides(even, e1, o1, 0), sides(even, m.at[:1], m.at[1:], 0)))
    for i in range(tile):
        logs[i + 1] = jnp.log(c_ref[i])
    for s, at, own in ((0, 0, 1), (1, tile + 1, tile)):
        logs[at] = jnp.where(halo[s][2], jnp.log(halo[s][1]), logs[own])
    ends = (
        jnp.where(halo[0][2], halo[0][0], v_ref[0]),
        jnp.where(halo[1][2], halo[1][0], v_ref[tile - 1]),
    )
    for i in range(tile):
        below = v_ref[i - 1] if i > 0 else ends[0]
        above = v_ref[i + 1] if i < tile - 1 else ends[1]
        vx = (above - below) * 0.5
        lx = (logs[i + 2] - logs[i]) * 0.5
        p, q, r, t = shifts(v_ref[i], True)
        vy, vz = (q - p) * 0.5, (t - r) * 0.5
        p, q, r, t = shifts(logs[i + 1], True)
        ly, lz = (q - p) * 0.5, (t - r) * 0.5
        ca = vy * lz - vz * ly
        cb = vz * lx - vx * lz
        cc = vx * ly - vy * lx
        out_ref[i] = penalty_gain * (ca * ca + cb * cb + cc * cc)


def weigh_kernel(mine, other, out_ref):
    tile, ny = out_ref.shape[1:3]
    for ref in (mine, other):
        label = jnp.broadcast_to(ref[tile * ny:tile * ny + 1], out_ref.shape[2:])
        for i in range(tile):
            acc = ref[i * ny:(i + 1) * ny]
            if ref is mine:
                out_ref[0, i] = label * acc
                out_ref[1, i] = (1.0 - label) * acc
            else:
                out_ref[0, i] += label * acc
                out_ref[1, i] += (1.0 - label) * acc


def renew_kernel(scale, meta, p_ref, q_ref, pen_ref, v_ref, c_ref, m_ref, coef_ref, e_ref, o_ref):
    a = meta[0].astype(F32)
    even = meta[1] == 0
    tile = v_ref.shape[0]
    for i in range(tile):
        new = []
        for n, ref in enumerate((v_ref, c_ref)):
            grad = scale * (p_ref[n, i] + q_ref[n, i])
            new.append(ref[i] * jnp.exp(-step_size * jnp.tanh(grad + pen_ref[i])))
            m_ref[n, i] = new[n]
        coef_ref[i] = coefficient(a, *new)
    for k in range(2):
        low, high = coef_ref[k], coef_ref[tile - 2 + k]
        e_ref[k] = jnp.where(even, high, low)
        o_ref[k] = jnp.where(even, low, high)


def second_kernel(meta, st_ref, hb_ref, hc_ref, re, ro, coef_ref, ce, co, out_ref, s3, s4, s5):
    a = meta[0].astype(F32)
    even = meta[1] == 0
    tile = st_ref.shape[2]
    _, flat = plane_tools(st_ref.shape[3:])
    far, near = sides(even, ce, co, 0), sides(even, ce, co, 1)
    cn = {-2: far[0], -1: near[0], tile: far[1], tile + 1: near[1]}

    def coef(j):
        return coef_ref[j] if 0 <= j < tile else cn[j]

    def lap(ref, j, off):
        return flat(ref[j + off]) + (ref[j + off - 1] + ref[j + off + 1])

    for n in range(2):
        two = sides(even, re, ro, 3 * n)
        s3[2], s3[tile + 3] = (hb_ref[s, n, 1] + hc_ref[s] * two[s] for s in range(2))
        s3[1], s3[tile + 4] = sides(even, re, ro, 3 * n + 1)
        s3[0], s3[tile + 5] = sides(even, re, ro, 3 * n + 2)
        prev = {-2: two[0], -1: hb_ref[0, n, 0], tile: hb_ref[1, n, 0], tile + 1: two[1]}
        for i in range(tile):
            s3[i + 3] = st_ref[n, 1, i]
        for j in range(-2, tile + 2):
            before = st_ref[n, 0, j] if 0 <= j < tile else prev[j]
            s4[j + 2] = (1.0 + a) * s3[j + 3] - a * before + coef(j) * lap(s3, j, 3)
        for j in range(-1, tile + 1):
            s5[j + 1] = (1.0 + a) * s4[j + 2] - a * s3[j + 3] + coef(j) * lap(s4, j, 2)
        for j in range(tile):
            out_ref[0, n, j] = (1.0 + a) * s5[j + 1] - a * s4[j + 2] + coef(j) * lap(s5, j, 1)


def swap_pairs(even_block, odd_block):
    count = lax.axis_size("space")
    evens = [(i, i ^ 1) for i in range(count) if i ^ 1 < count]
    odds = [(i, ((i + 1) ^ 1) - 1) for i in range(count) if 0 <= ((i + 1) ^ 1) - 1 < count]
    return lax.ppermute(even_block, "space", evens), lax.ppermute(odd_block, "space", odds)


def across(block, mask):
    count = lax.axis_size("src")
    return lax.ppermute(block, "src", [(i, i ^ mask) for i in range(count)])


def block_step(fields, velocity, conductivity, labels):
    tile, ny, nz = velocity.shape
    plane = (ny, nz)
    here, count = lax.axis_index("space"), lax.axis_size("space")
    core = lax.axis_index("src") % 2
    meta = jnp.stack(
        [
            labels[0],
            here % 2,
            (here > 0).astype(jnp.int32),
            (here < count - 1).astype(jnp.int32),
            core,
        ]
    )
    even = here % 2 == 0

    edges = []
    for at in (0, tile - 1):
        model = jnp.where(core == 0, velocity[at], conductivity[at])
        edges.append(jnp.stack([model, fields[0, 0, at], fields[0, 2, at]], 0))
    low, high = edges
    e1, o1 = swap_pairs(jnp.where(even, high, low), jnp.where(even, low, high))

    stack = pltpu.VMEM((tile, *plane), F32)
    e2, o2, coef = call(
        isolated_kernel,
        [(4, *plane), (4, *plane), (tile, *plane)],
        (meta, fields, velocity, conductivity),
        [SMEM, VMEM, VMEM, VMEM],
        [stack, stack],
    )
    e2, o2 = swap_pairs(e2, o2)
    (other,) = call(pick_kernel, [(2, *plane)], (e1, o1), [VMEM] * 2)
    other = across(other, 1)

    acc, state, halo, halo_coef, e3, o3 = call(
        first_kernel,
        [
            (tile * ny + 8, nz),
            (2, 2, tile, *plane),
            (2, 2, 2, *plane),
            (2, *plane),
            (6, *plane),
            (6, *plane),
        ],
        (meta, fields, coef, e1, o1, other, e2, o2),
        [SMEM] + [VMEM] * 7,
        [pltpu.VMEM((2, tile, *plane), F32)],
    )

    groups = lax.axis_size("src")
    masks = [1 << k for k in reversed(range(groups.bit_length() - 1))]
    acc_other = across(acc, masks[0])
    e3, o3 = swap_pairs(e3, o3)
    (pen,) = call(
        penalty_kernel,
        [(tile, *plane)],
        (meta, velocity, conductivity, e1, o1, other),
        [SMEM] + [VMEM] * 5,
        [pltpu.VMEM((tile + 2, *plane), F32)],
    )
    (part,) = call(weigh_kernel, [(2, tile, *plane)], (acc, acc_other), [VMEM] * 2)
    for mask in masks[1:-1]:
        part = part + across(part, mask)
    rest = across(part, masks[-1])

    scale = 1.0 / (20.0 * math.sqrt(groups * labels.shape[0]))
    models, coef_next, e4, o4 = call(
        lambda *refs: renew_kernel(scale, *refs),
        [(2, tile, *plane), (tile, *plane), (2, *plane), (2, *plane)],
        (meta, part, rest, pen, velocity, conductivity),
        [SMEM] + [VMEM] * 5,
    )
    e4, o4 = swap_pairs(e4, o4)
    (final,) = call(
        second_kernel,
        [(1, 2, tile, *plane)],
        (meta, state, halo, halo_coef, e3, o3, coef_next, e4, o4),
        [SMEM] + [VMEM] * 8,
        [
            pltpu.VMEM((tile + 6, *plane), F32),
            pltpu.VMEM((tile + 4, *plane), F32),
            pltpu.VMEM((tile + 2, *plane), F32),
        ],
    )
    return final, models


def solution(mesh):
    in_specs = (
        P(("parts", "src"), None, "space", None, None),
        P(("parts", "space"), None, None),
        P(("parts", "space"), None, None),
        P(("parts", "src")),
    )
    out_specs = (
        P(("parts", "src"), None, "space", None, None),
        P(None, ("parts", "space"), None, None),
    )
    return jax.shard_map(
        block_step, mesh=mesh, in_specs=in_specs, out_specs=out_specs, check_vma=False
    )
```

```python
import math

import jax
import jax.numpy as jnp
from jax import lax
from jax.experimental import pallas as pl
from jax.experimental.pallas import tpu as pltpu
from jax.sharding import PartitionSpec as P


speed_gain = 0.25
diffuse_gain = 0.15
step_size = 0.1
penalty_gain = 50.0

VMEM = pl.BlockSpec(memory_space=pltpu.VMEM)
F32 = jnp.float32


def call(kernel, outs, args, scratch=(), specs=None, extra=()):
    size = sum(math.prod(o) for o in outs) + sum(a.size for a in args)
    return pl.pallas_call(
        kernel,
        out_shape=tuple(jax.ShapeDtypeStruct(o, F32) for o in outs),
        in_specs=specs or [VMEM for _ in args],
        out_specs=tuple(VMEM for _ in outs),
        scratch_shapes=[pltpu.VMEM(s, F32) for s in scratch] + list(extra),
        compiler_params=pltpu.CompilerParams(vmem_limit_bytes=16 << 20),
        cost_estimate=pl.CostEstimate(flops=20 * size, bytes_accessed=4 * size, transcendentals=0),
    )(*args)


class Plane:
    def __init__(self, ref, *at, base=0):
        self.ref, self.at, self.base = ref, at, base

    def _rows(self, r, n):
        return (*self.at, slice(self.base + r, self.base + r + n))

    def get(self, r, n):
        return self.ref[self._rows(r, n)]

    def put(self, r, n, value):
        self.ref[self._rows(r, n)] = value


class Work:
    def __init__(self, weight_ref, ny, nz):
        self.ny, self.n = ny, 32 if ny % 32 == 0 else ny
        shape = (self.n, nz)
        row = lax.broadcasted_iota(jnp.int32, shape, 0)
        col = lax.broadcasted_iota(jnp.int32, shape, 1)
        self.top, self.bottom = row == 0, row == self.n - 1
        self.left, self.right = col == 0, col == nz - 1
        self.nz = nz
        if weight_ref is not None:
            self.a = jnp.broadcast_to(weight_ref[0:1], shape)
        here = lax.axis_index("space")
        self.even = here % 2 == 0
        self.has = (here > 0, here < lax.axis_size("space") - 1)
        self.first_core = lax.axis_index("src") % 2 == 0

    def blocks(self):
        return range(0, self.ny, self.n)

    def get(self, plane, r):
        return plane.get(r, self.n)

    def put(self, plane, r, value):
        plane.put(r, self.n, value)

    def shifts(self, plane, r, edge):
        n, v = self.n, plane.get(r, self.n)

        def fill(test, moved):
            return jnp.where(test, v if edge else 0.0, moved)

        up = plane.get(r - 1, n) if r > 0 else fill(self.top, pltpu.roll(v, 1, 0))
        last = r + n == self.ny
        down = fill(self.bottom, pltpu.roll(v, n - 1, 0)) if last else plane.get(r + 1, n)
        left = fill(self.left, pltpu.roll(v, 1, 1))
        right = fill(self.right, pltpu.roll(v, self.nz - 1, 1))
        return v, up, down, left, right

    def flat(self, plane, r):
        v, up, down, left, right = self.shifts(plane, r, False)
        return v, ((up + down) + (left + right)) - 6.0 * v

    def lap(self, plane, below, above, r):
        v, total = self.flat(plane, r)
        for other in (below, above):
            if other is not None:
                total = total + self.get(other, r)
        return v, total

    def ahead(self, v, before):
        return (1.0 + self.a) * v - self.a * before

    def step(self, out, now, before, coef, below, above, each=None):
        for r in self.blocks():
            v, total = self.lap(now, below, above, r)
            value = self.ahead(v, self.get(before, r)) + self.get(coef, r) * total
            if out is not None:
                self.put(out, r, value)
            if each is not None:
                each(r, v, total, value)

    def coefficient(self, v, c):
        return self.a * speed_gain * v**2 + (1.0 - self.a) * diffuse_gain / c

    def pack(self, even_ref, odd_ref, lows, highs):
        for k, (low, high) in enumerate(zip(lows, highs)):
            for r in self.blocks():
                lo, hi = self.get(low, r), self.get(high, r)
                self.put(Plane(even_ref, k), r, jnp.where(self.even, hi, lo))
                self.put(Plane(odd_ref, k), r, jnp.where(self.even, lo, hi))

    def unpack(self, even_ref, odd_ref, k, r):
        e, o = self.get(Plane(even_ref, k), r), self.get(Plane(odd_ref, k), r)
        return jnp.where(self.even, o, e), jnp.where(self.even, e, o)


def near(make, i, tile, ends=(None, None)):
    return (make(i - 1) if i > 0 else ends[0]), (make(i + 1) if i < tile - 1 else ends[1])


def isolated_kernel(
    labels, f_in, v_in, c_in,
    ae, ao, be, bo, ce, co, coef, one, acc, w, f, v, c, two, label, sems,
):
    copies = [
        pltpu.make_async_copy(src, dst, sems.at[n])
        for n, (src, dst) in enumerate(((labels, label), (v_in, v), (c_in, c), (f_in, f)))
    ]
    for copy in copies:
        copy.start()
    tile, ny, nz = v.shape
    copies[0].wait()
    w[...] = jnp.full(w.shape, label[0].astype(F32), F32)
    k = Work(w, ny, nz)
    copies[1].wait()
    copies[2].wait()
    edge = (0, tile - 1)
    for i in range(tile):
        for r in k.blocks():
            k.put(Plane(coef, i), r, k.coefficient(v[i, r:r + k.n], c[i, r:r + k.n]))
    copies[3].wait()
    for n in range(2):
        for i in range(tile):

            def each(r, value, total, out, i=i):
                k.put(Plane(acc, i), r, f[0, 2, i, r:r + k.n] * total)

            k.step(
                Plane(one, n, i), Plane(f, 0, 2 * n, i), Plane(f, 0, 2 * n + 1, i), Plane(coef, i),
                *near(lambda j: Plane(f, 0, 2 * n, j), i, tile), each if n == 0 else None,
            )
        for s, i in enumerate(edge):
            k.step(
                Plane(two, n, s), Plane(one, n, i), Plane(f, 0, 2 * n, i), Plane(coef, i),
                *near(lambda j: Plane(one, n, j), i, tile),
            )
    sides = [
        [Plane(coef, i), Plane(f, 0, 0, i), Plane(f, 0, 2, i), Plane(one, 0, i)] for i in edge
    ]
    k.pack(ae, ao, *sides)
    k.pack(be, bo, *([Plane(two, 0, s), Plane(one, 1, i)] for s, i in enumerate(edge)))
    for r in k.blocks():
        lo, hi = (
            jnp.where(k.first_core, v[i, r:r + k.n], c[i, r:r + k.n]) for i in edge
        )
        k.put(Plane(ce, 0), r, jnp.where(k.even, hi, lo))
        k.put(Plane(co, 0), r, jnp.where(k.even, lo, hi))
    k.pack(ce.at[1:], co.at[1:], [Plane(two, 1, 0)], [Plane(two, 1, 1)])


def inner_kernel(w, f, coef, one, acc, ae, ao, acc1, rim, ends, two, three, halo, zero):
    tile, ny, nz = coef.shape
    k = Work(w, ny, nz)
    edge = (0, tile - 1)
    for r in k.blocks():
        parts = [k.unpack(ae, ao, m, r) for m in range(4)]
        for s, i in enumerate(edge):
            h = [p[s] for p in parts]
            cf, w0, u0 = coef[i, r:r + k.n], f[0, 2, i, r:r + k.n], f[0, 0, i, r:r + k.n]
            k.put(Plane(halo, s, 0), r, h[0])
            k.put(Plane(halo, s, 1), r, h[3] + h[0] * u0)
            k.put(Plane(ends, 0, s), r, one[0, i, r:r + k.n] + cf * h[1])
            k.put(Plane(ends, 1, s), r, one[1, i, r:r + k.n] + cf * h[2])
            k.put(Plane(zero, s), r, acc[i, r:r + k.n] + w0 * h[1])

    def first(n, i):
        return Plane(ends, n, edge.index(i)) if i in edge else Plane(one, n, i)

    def inside(i):
        return Plane(acc1, base=(i - 1) * ny)

    outside = (Plane(halo, 0, 1), Plane(halo, 1, 1))
    for i in range(tile):

        def each(r, value, total, out, i=i):
            term = k.get(first(1, i), r) * total
            if i in edge:
                s = edge.index(i)
                k.put(Plane(rim, s), r, zero[s, r:r + k.n] + term)
            else:
                k.put(inside(i), r, acc[i, r:r + k.n] + term)

        k.step(
            Plane(two, 0, i), first(0, i), Plane(f, 0, 0, i), Plane(coef, i),
            *near(lambda j: first(0, j), i, tile, outside), each,
        )
    for i in range(1, tile - 1):
        k.step(
            Plane(two, 1, i), first(1, i), Plane(f, 0, 2, i), Plane(coef, i),
            *near(lambda j: first(1, j), i, tile),
        )
    for i in range(1, tile - 1):

        def each(r, value, total, out, i=i):
            k.put(inside(i), r, k.get(inside(i), r) + two[1, i, r:r + k.n] * total)

        k.step(
            Plane(three, i), Plane(two, 0, i), first(0, i), Plane(coef, i),
            *near(lambda j: Plane(two, 0, j), i, tile), each,
        )
    rows = (tile - 2) * ny
    acc1[rows:] = jnp.broadcast_to(w[0:1], (acc1.shape[0] - rows, nz))
    for i in edge:
        for r in k.blocks():
            k.put(Plane(two, 1, i), r, jnp.zeros((k.n, nz), F32))


def outer_kernel(w, f, coef, one, ends, two, halo, rim, be, bo, acc2, wtwo, uthree, beyond, d):
    tile, ny, nz = coef.shape
    k = Work(w, ny, nz)
    edge = (0, tile - 1)
    for s, i in enumerate(edge):
        for r in k.blocks():
            k.put(Plane(d, s), r, halo[s, 0, r:r + k.n] * f[0, 0, i, r:r + k.n])
    for r in k.blocks():
        u2, w1 = k.unpack(be, bo, 0, r), k.unpack(be, bo, 1, r)
        for s, i in enumerate(edge):
            h = halo[s, 0, r:r + k.n]
            dv, total = k.flat(Plane(d, s), r)
            total = total + ends[0, s, r:r + k.n]
            k.put(Plane(beyond, s, 0), r, u2[s] + (1.0 + k.a) * dv + h * total)
            k.put(Plane(beyond, s, 1), r, w1[s] + h * f[0, 2, i, r:r + k.n])

    def first(n, i):
        return Plane(ends, n, edge.index(i)) if i in edge else Plane(one, n, i)

    for s, i in enumerate(edge):
        k.step(
            Plane(wtwo, s), first(1, i), Plane(f, 0, 2, i), Plane(coef, i),
            *near(lambda j: first(1, j), i, tile, (Plane(beyond, 0, 1), Plane(beyond, 1, 1))),
        )

        def each(r, value, total, out, s=s):
            k.put(
                Plane(acc2, base=s * ny), r,
                rim[s, r:r + k.n] + wtwo[s, r:r + k.n] * total,
            )

        k.step(
            Plane(uthree, s), Plane(two, 0, i), first(0, i), Plane(coef, i),
            *near(lambda j: Plane(two, 0, j), i, tile, (Plane(beyond, 0, 0), Plane(beyond, 1, 0))),
            each,
        )


def early_kernel(w, coef, one, ends, two, wtwo, three, uthree, pe, po, wthree):
    tile, ny, nz = coef.shape
    k = Work(w, ny, nz)
    edge = (0, tile - 1)

    def second(i):
        return Plane(wtwo, edge.index(i)) if i in edge else Plane(two, 1, i)

    for i in range(1, tile - 1):
        k.step(
            Plane(wthree, i - 1), second(i), Plane(one, 1, i), Plane(coef, i),
            *near(second, i, tile),
        )

    def planes(i, j):
        return [
            Plane(two, 0, i), Plane(three, i), Plane(three, j),
            Plane(two, 1, i), Plane(wthree, i - 1), Plane(wthree, j - 1),
        ]

    k.pack(pe, po, planes(1, 2), planes(tile - 2, tile - 3))


def pick_kernel(ce, co, out):
    out[0], out[1] = ce[0], co[0]


def late_kernel(
    w, v, c, f, coef, ends, two, wtwo, halo, beyond, ce, co, other,
    pen, wthree, base, last, logs, rims, d,
):
    tile, ny, nz = coef.shape
    k = Work(w, ny, nz)
    edge = (0, tile - 1)
    for i in range(tile):
        for r in k.blocks():
            k.put(Plane(logs, i + 1), r, jnp.log(c[i, r:r + k.n]))
    for r in k.blocks():
        mine = k.unpack(ce, co, 0, r)
        theirs = k.unpack(other.at[0:1], other.at[1:2], 0, r)
        w2 = k.unpack(ce, co, 1, r)
        for s, i in enumerate(edge):
            vel = jnp.where(k.first_core, mine[s], theirs[s])
            con = jnp.where(k.first_core, theirs[s], mine[s])
            con = jnp.where(k.has[s], con, 1.0)
            k.put(Plane(rims, s), r, jnp.where(k.has[s], vel, v[i, r:r + k.n]))
            k.put(
                Plane(logs, (0, tile + 1)[s]), r,
                jnp.where(k.has[s], jnp.log(con), logs[i + 1, r:r + k.n]),
            )
            k.put(Plane(d, s), r, halo[s, 0, r:r + k.n] * f[0, 2, i, r:r + k.n])
            k.put(Plane(last, s), r, w2[s])
    for s, i in enumerate(edge):
        for r in k.blocks():
            dv, total = k.flat(Plane(d, s), r)
            total = total + ends[1, s, r:r + k.n]
            k.put(
                Plane(last, s), r,
                last[s, r:r + k.n] + (1.0 + k.a) * dv + halo[s, 0, r:r + k.n] * total,
            )

    def second(i):
        return Plane(wtwo, edge.index(i)) if i in edge else Plane(two, 1, i)

    for s, i in enumerate(edge):
        k.step(
            Plane(wthree, s), second(i), Plane(ends, 1, s), Plane(coef, i),
            *near(second, i, tile, (Plane(last, 0), Plane(last, 1))),
        )
        k.step(
            Plane(base, s, 0), Plane(beyond, s, 0), Plane(halo, s, 1), Plane(halo, s, 0),
            Plane(two, 0, i), None,
        )
        k.step(
            Plane(base, s, 1), Plane(last, s), Plane(beyond, s, 1), Plane(halo, s, 0),
            Plane(wtwo, s), None,
        )
    for i in range(tile):
        below, above = near(lambda j: Plane(v, j), i, tile, (Plane(rims, 0), Plane(rims, 1)))
        for r in k.blocks():
            vx = (k.get(above, r) - k.get(below, r)) * 0.5
            lx = (logs[i + 2, r:r + k.n] - logs[i, r:r + k.n]) * 0.5
            _, up, down, left, right = k.shifts(Plane(v, i), r, True)
            vy, vz = (down - up) * 0.5, (right - left) * 0.5
            _, up, down, left, right = k.shifts(Plane(logs, i + 1), r, True)
            ly, lz = (down - up) * 0.5, (right - left) * 0.5
            ca = vy * lz - vz * ly
            cb = vz * lx - vx * lz
            cc = vx * ly - vy * lx
            k.put(Plane(pen, i), r, penalty_gain * (ca * ca + cb * cb + cc * cc))


def weigh_kernel(acc1, acc2, far1, far2, out):
    _, tile, ny, nz = out.shape
    k = Work(None, ny, nz)
    rows = (tile - 2) * ny
    labels = [jnp.broadcast_to(ref[rows:rows + 1], (k.n, nz)) for ref in (acc1, far1)]
    for i in range(tile):
        for r in k.blocks():
            if i in (0, tile - 1):
                at = (0 if i == 0 else ny) + r
                mine, other = acc2[at:at + k.n], far2[at:at + k.n]
            else:
                at = (i - 1) * ny + r
                mine, other = acc1[at:at + k.n], far1[at:at + k.n]
            k.put(Plane(out, 0, i), r, labels[0] * mine + labels[1] * other)
            k.put(Plane(out, 1, i), r, (1.0 - labels[0]) * mine + (1.0 - labels[1]) * other)


def renew(scale, value, part, rest, pen):
    return value * jnp.exp(-step_size * jnp.tanh(scale * (part + rest) + pen))


def renew_kernel(scale, w, part, rest, pen, v, c, coef, e, o):
    tile, ny, nz = v.shape
    k = Work(w, ny, nz)
    sound = k.a == 1.0
    for i in range(tile):
        for r in k.blocks():
            at = slice(r, r + k.n)
            new = renew(
                scale,
                jnp.where(sound, v[i, at], c[i, at]),
                jnp.where(sound, part[0, i, at], part[1, i, at]),
                jnp.where(sound, rest[0, i, at], rest[1, i, at]),
                pen[i, at],
            )
            k.put(
                Plane(coef, i), r,
                jnp.where(sound, speed_gain * new**2, diffuse_gain / new),
            )
    k.pack(e, o, [Plane(coef, 0), Plane(coef, 1)], [Plane(coef, tile - 2), Plane(coef, tile - 1)])


def models_kernel(scale, part, rest, pen, v, c, out):
    tile, ny, nz = v.shape
    k = Work(None, ny, nz)
    for n, ref in enumerate((v, c)):
        for i in range(tile):
            for r in k.blocks():
                at = slice(r, r + k.n)
                out[n, i, at] = renew(scale, ref[i, at], part[n, i, at], rest[n, i, at], pen[i, at])


def before_kernel(
    w, coef, two, wtwo, three, uthree, winner, wthree, base, halo, beyond, last, pe, po,
    four, five, ring, lap, side, wide, prev,
):
    tile, ny, nz = coef.shape
    k = Work(w, ny, nz)
    edge = (0, tile - 1)
    for n in range(2):
        for r in k.blocks():
            at = slice(r, r + k.n)
            two_far = k.unpack(pe, po, 3 * n, r)
            three_far = k.unpack(pe, po, 3 * n + 1, r)
            three_end = k.unpack(pe, po, 3 * n + 2, r)
            for s in range(2):
                third = base[s, n, at] + halo[s, 0, at] * two_far[s]
                side[n, s, at] = third
                wide[(2, tile + 3)[s], at] = third
                wide[(1, tile + 4)[s], at] = three_far[s]
                wide[(0, tile + 5)[s], at] = three_end[s]
                prev[s, at] = two_far[s]

        def third_plane(i):
            if i in edge:
                return Plane(wthree if n else uthree, edge.index(i))
            return Plane(winner, i - 1) if n else Plane(three, i)

        for i in range(tile):
            for r in k.blocks():
                k.put(Plane(wide, i + 3), r, k.get(third_plane(i), r))

        def second(i):
            return Plane(wtwo, edge.index(i)) if n and i in edge else Plane(two, n, i)

        for i in range(tile):
            k.step(
                Plane(four, n, i), Plane(wide, i + 3), second(i), Plane(coef, i),
                Plane(wide, i + 2), Plane(wide, i + 4),
            )
        for s in range(2):
            for m, j in enumerate(((-2, -1), (tile + 1, tile))[s]):
                known = Plane(last, s) if n else Plane(beyond, s, 0)
                earlier = known if m else Plane(prev, s)
                for r in k.blocks():
                    value, total = k.lap(Plane(wide, j + 3), Plane(wide, j + 2), Plane(wide, j + 4), r)
                    k.put(Plane(ring, n, s, m), r, k.ahead(value, k.get(earlier, r)))
                    k.put(Plane(lap, n, s, m), r, total)
        for i in range(1, tile - 1):
            k.step(
                Plane(five, n, i - 1), Plane(four, n, i), third_plane(i), Plane(coef, i),
                Plane(four, n, i - 1), Plane(four, n, i + 1),
            )


def after_kernel(w, coef, four, five, ring, lap, side, uthree, wthree, e, o, out, cn, far, ends):
    tile, ny, nz = coef.shape
    k = Work(w, ny, nz)
    edge = (0, tile - 1)
    for r in k.blocks():
        parts = [k.unpack(e, o, m, r) for m in range(2)]
        for s in range(2):
            order = (0, 1) if s == 0 else (1, 0)
            for m in range(2):
                k.put(Plane(cn, s, m), r, parts[order[m]][s])
    for n in range(2):
        for s in range(2):
            for m in range(2):
                for r in k.blocks():
                    at = slice(r, r + k.n)
                    far[s, m, at] = ring[n, s, m, at] + cn[s, m, at] * lap[n, s, m, at]
        for s, i in enumerate(edge):
            k.step(
                Plane(ends, s, 0), Plane(far, s, 1), Plane(side, n, s), Plane(cn, s, 1),
                Plane(far, s, 0), Plane(four, n, i),
            )
            k.step(
                Plane(ends, s, 1), Plane(four, n, i), Plane(wthree if n else uthree, s),
                Plane(coef, i),
                *near(lambda j: Plane(four, n, j), i, tile, (Plane(far, 0, 1), Plane(far, 1, 1))),
            )

        def fifth(i):
            return Plane(ends, edge.index(i), 1) if i in edge else Plane(five, n, i - 1)

        for i in range(tile):
            k.step(
                Plane(out, 0, n, i), fifth(i), Plane(four, n, i), Plane(coef, i),
                *near(fifth, i, tile, (Plane(ends, 0, 0), Plane(ends, 1, 0))),
            )


def swap_pairs(even_block, odd_block):
    count = lax.axis_size("space")
    evens = [(i, i ^ 1) for i in range(count) if i ^ 1 < count]
    odds = [(i, ((i + 1) ^ 1) - 1) for i in range(count) if 0 <= ((i + 1) ^ 1) - 1 < count]
    return lax.ppermute(even_block, "space", evens), lax.ppermute(odd_block, "space", odds)


def across(block, mask):
    count = lax.axis_size("src")
    return lax.ppermute(block, "src", [(i, i ^ mask) for i in range(count)])


def block_step(fields, velocity, conductivity, labels):
    tile, ny, nz = velocity.shape
    groups = lax.axis_size("src")
    assert tile >= 4 and labels.shape[0] == 1 and groups >= 4 and groups & (groups - 1) == 0
    scale = 1.0 / (20.0 * math.sqrt(groups))

    def planes(*lead):
        return (*lead, ny, nz)

    ae, ao, be, bo, ce, co, coef, one, acc, w, fields, velocity, conductivity = call(
        isolated_kernel,
        [planes(4)] * 2 + [planes(2)] * 4 + [planes(tile), planes(2, tile), planes(tile)]
        + [(8, nz), fields.shape, velocity.shape, conductivity.shape],
        (labels, fields, velocity, conductivity),
        [planes(2, 2)],
        [pl.BlockSpec(memory_space=pltpu.HBM)] * 4,
        [pltpu.SMEM((1,), jnp.int32), pltpu.SemaphoreType.DMA((4,))],
    )
    ae, ao = swap_pairs(ae, ao)
    be, bo = swap_pairs(be, bo)
    ce, co = swap_pairs(ce, co)

    acc1, rim, ends, two, three, halo = call(
        inner_kernel,
        [((tile - 2) * ny + 8, nz), planes(2), planes(2, 2), planes(2, tile), planes(tile), planes(2, 2)],
        (w, fields, coef, one, acc, ae, ao),
        [planes(2)],
    )
    masks = [1 << k for k in reversed(range(groups.bit_length() - 1))]
    far1 = across(acc1, masks[0])
    acc2, wtwo, uthree, beyond = call(
        outer_kernel,
        [(2 * ny, nz), planes(2), planes(2), planes(2, 2)],
        (w, fields, coef, one, ends, two, halo, rim, be, bo),
        [planes(2)],
    )
    far2 = across(acc2, masks[0])
    pe, po, winner = call(
        early_kernel,
        [planes(6), planes(6), planes(tile - 2)],
        (w, coef, one, ends, two, wtwo, three, uthree),
    )
    pe, po = swap_pairs(pe, po)
    (other,) = call(pick_kernel, [planes(2)], (ce, co))
    other = across(other, 1)

    (part,) = call(weigh_kernel, [planes(2, tile)], (acc1, acc2, far1, far2))
    for mask in masks[1:-1]:
        part = part + across(part, mask)
    rest = across(part, masks[-1])
    pen, wthree, base, last = call(
        late_kernel,
        [planes(tile), planes(2), planes(2, 2), planes(2)],
        (w, velocity, conductivity, fields, coef, ends, two, wtwo, halo, beyond, ce, co, other),
        [planes(tile + 2), planes(2), planes(2)],
    )
    coef_next, e, o = call(
        lambda *refs: renew_kernel(scale, *refs),
        [planes(tile), planes(2), planes(2)],
        (w, part, rest, pen, velocity, conductivity),
    )
    e, o = swap_pairs(e, o)
    (models,) = call(
        lambda *refs: models_kernel(scale, *refs),
        [planes(2, tile)], (part, rest, pen, velocity, conductivity),
    )
    four, five, ring, lap, side = call(
        before_kernel,
        [planes(2, tile), planes(2, tile - 2), planes(2, 2, 2), planes(2, 2, 2), planes(2, 2)],
        (w, coef_next, two, wtwo, three, uthree, winner, wthree, base, halo, beyond, last, pe, po),
        [planes(tile + 6), planes(2)],
    )
    (final,) = call(
        after_kernel,
        [planes(1, 2, tile)],
        (w, coef_next, four, five, ring, lap, side, uthree, wthree, e, o),
        [planes(2, 2), planes(2, 2), planes(2, 2)],
    )
    return final, models


def solution(mesh):
    in_specs = (
        P(("parts", "src"), None, "space", None, None),
        P(("parts", "space"), None, None),
        P(("parts", "space"), None, None),
        P(("parts", "src")),
    )
    out_specs = (
        P(("parts", "src"), None, "space", None, None),
        P(None, ("parts", "space"), None, None),
    )
    return jax.shard_map(
        block_step, mesh=mesh, in_specs=in_specs, out_specs=out_specs, check_vma=False
    )
```

```python
import math

import jax
import jax.numpy as jnp
from jax import lax
from jax.experimental import pallas as pl
from jax.experimental.pallas import tpu as pltpu
from jax.sharding import PartitionSpec as P


speed_gain = 0.25
diffuse_gain = 0.15
step_size = 0.1
penalty_gain = 50.0

VMEM = pl.BlockSpec(memory_space=pltpu.VMEM)
F32 = jnp.float32


def call(kernel, outs, args, scratch=(), specs=None, extra=(), out_spec=VMEM):
    size = sum(math.prod(o) for o in outs) + sum(a.size for a in args)
    return pl.pallas_call(
        kernel,
        out_shape=tuple(jax.ShapeDtypeStruct(o, F32) for o in outs),
        in_specs=specs or [VMEM for _ in args],
        out_specs=tuple(out_spec for _ in outs),
        scratch_shapes=[pltpu.VMEM(s, F32) for s in scratch] + list(extra),
        compiler_params=pltpu.CompilerParams(vmem_limit_bytes=16 << 20),
        cost_estimate=pl.CostEstimate(flops=20 * size, bytes_accessed=4 * size, transcendentals=0),
    )(*args)


class Plane:
    def __init__(self, ref, *at, base=0):
        self.ref, self.at, self.base = ref, at, base

    def _rows(self, r, n):
        return (*self.at, slice(self.base + r, self.base + r + n))

    def get(self, r, n):
        return self.ref[self._rows(r, n)]

    def put(self, r, n, value):
        self.ref[self._rows(r, n)] = value


class Work:
    def __init__(self, weight_ref, ny, nz):
        self.ny, self.n = ny, 32 if ny % 32 == 0 else ny
        shape = (self.n, nz)
        row = lax.broadcasted_iota(jnp.int32, shape, 0)
        col = lax.broadcasted_iota(jnp.int32, shape, 1)
        self.top, self.bottom = row == 0, row == self.n - 1
        self.left, self.right = col == 0, col == nz - 1
        self.nz = nz
        if weight_ref is not None:
            self.a = jnp.broadcast_to(weight_ref[0:1], shape)
        here = lax.axis_index("space")
        self.even = here % 2 == 0
        self.has = (here > 0, here < lax.axis_size("space") - 1)
        self.first_core = lax.axis_index("src") % 2 == 0

    def blocks(self):
        return range(0, self.ny, self.n)

    def get(self, plane, r):
        return plane.get(r, self.n)

    def put(self, plane, r, value):
        plane.put(r, self.n, value)

    def shifts(self, plane, r, edge):
        n, v = self.n, plane.get(r, self.n)

        def fill(test, moved):
            return jnp.where(test, v if edge else 0.0, moved)

        up = plane.get(r - 1, n) if r > 0 else fill(self.top, pltpu.roll(v, 1, 0))
        last = r + n == self.ny
        down = fill(self.bottom, pltpu.roll(v, n - 1, 0)) if last else plane.get(r + 1, n)
        left = fill(self.left, pltpu.roll(v, 1, 1))
        right = fill(self.right, pltpu.roll(v, self.nz - 1, 1))
        return v, up, down, left, right

    def flat(self, plane, r):
        v, up, down, left, right = self.shifts(plane, r, False)
        return v, ((up + down) + (left + right)) - 6.0 * v

    def lap(self, plane, below, above, r):
        v, total = self.flat(plane, r)
        for other in (below, above):
            if other is not None:
                total = total + self.get(other, r)
        return v, total

    def ahead(self, v, before):
        return (1.0 + self.a) * v - self.a * before

    def step(self, out, now, before, coef, below, above, each=None):
        for r in self.blocks():
            v, total = self.lap(now, below, above, r)
            value = self.ahead(v, self.get(before, r)) + self.get(coef, r) * total
            if out is not None:
                self.put(out, r, value)
            if each is not None:
                each(r, v, total, value)

    def coefficient(self, v, c):
        return self.a * speed_gain * v**2 + (1.0 - self.a) * diffuse_gain / c

    def pack(self, even_ref, odd_ref, lows, highs):
        for k, (low, high) in enumerate(zip(lows, highs)):
            for r in self.blocks():
                lo, hi = self.get(low, r), self.get(high, r)
                self.put(Plane(even_ref, k), r, jnp.where(self.even, hi, lo))
                self.put(Plane(odd_ref, k), r, jnp.where(self.even, lo, hi))

    def unpack(self, even_ref, odd_ref, k, r):
        e, o = self.get(Plane(even_ref, k), r), self.get(Plane(odd_ref, k), r)
        return jnp.where(self.even, o, e), jnp.where(self.even, e, o)


def near(make, i, tile, ends=(None, None)):
    return (make(i - 1) if i > 0 else ends[0]), (make(i + 1) if i < tile - 1 else ends[1])


def isolated_kernel(
    label, f_in, v_in, c_in,
    ae, ao, be, bo, coef, one, acc, w, f, v, c, two, sems,
):
    copies = [
        pltpu.make_async_copy(src, dst, sems.at[n])
        for n, (src, dst) in enumerate(((v_in, v), (c_in, c), (f_in, f)))
    ]
    for copy in copies:
        copy.start()
    tile, ny, nz = v.shape
    w[...] = jnp.full(w.shape, label[0].astype(F32), F32)
    k = Work(w, ny, nz)
    copies[0].wait()
    copies[1].wait()
    edge = (0, tile - 1)
    for i in range(tile):
        for r in k.blocks():
            k.put(Plane(coef, i), r, k.coefficient(v[i, r:r + k.n], c[i, r:r + k.n]))
    copies[2].wait()
    for n in range(2):
        for i in range(tile):

            def each(r, value, total, out, i=i):
                k.put(Plane(acc, i), r, f[0, 2, i, r:r + k.n] * total)

            k.step(
                Plane(one, n, i), Plane(f, 0, 2 * n, i), Plane(f, 0, 2 * n + 1, i), Plane(coef, i),
                *near(lambda j: Plane(f, 0, 2 * n, j), i, tile), each if n == 0 else None,
            )
    for s, i in enumerate(edge):
        k.step(
            Plane(two, s), Plane(one, 0, i), Plane(f, 0, 0, i), Plane(coef, i),
            *near(lambda j: Plane(one, 0, j), i, tile),
        )
    sides = [
        [Plane(coef, i), Plane(f, 0, 0, i), Plane(f, 0, 2, i), Plane(one, 0, i)] for i in edge
    ]
    k.pack(ae, ao, *sides)
    k.pack(be, bo, *([Plane(two, s), Plane(one, 1, i)] for s, i in enumerate(edge)))
    for r in k.blocks():
        lo, hi = (
            jnp.where(k.first_core, v[i, r:r + k.n], c[i, r:r + k.n]) for i in edge
        )
        k.put(Plane(be, 2), r, jnp.where(k.even, hi, lo))
        k.put(Plane(bo, 2), r, jnp.where(k.even, lo, hi))


def inner_kernel(w, f, coef, one, acc, ae, ao, acc1, rim, ends, two, three, halo, zero):
    tile, ny, nz = coef.shape
    k = Work(w, ny, nz)
    edge = (0, tile - 1)
    for r in k.blocks():
        parts = [k.unpack(ae, ao, m, r) for m in range(4)]
        for s, i in enumerate(edge):
            h = [p[s] for p in parts]
            cf, w0, u0 = coef[i, r:r + k.n], f[0, 2, i, r:r + k.n], f[0, 0, i, r:r + k.n]
            k.put(Plane(halo, s, 0), r, h[0])
            k.put(Plane(halo, s, 1), r, h[3] + h[0] * u0)
            k.put(Plane(ends, 0, s), r, one[0, i, r:r + k.n] + cf * h[1])
            k.put(Plane(ends, 1, s), r, one[1, i, r:r + k.n] + cf * h[2])
            k.put(Plane(zero, s), r, acc[i, r:r + k.n] + w0 * h[1])

    def first(n, i):
        return Plane(ends, n, edge.index(i)) if i in edge else Plane(one, n, i)

    def inside(i):
        return Plane(acc1, base=(i - 1) * ny)

    outside = (Plane(halo, 0, 1), Plane(halo, 1, 1))
    for i in range(tile):

        def each(r, value, total, out, i=i):
            term = k.get(first(1, i), r) * total
            if i in edge:
                s = edge.index(i)
                k.put(Plane(rim, s), r, zero[s, r:r + k.n] + term)
            else:
                k.put(inside(i), r, acc[i, r:r + k.n] + term)

        k.step(
            Plane(two, 0, i), first(0, i), Plane(f, 0, 0, i), Plane(coef, i),
            *near(lambda j: first(0, j), i, tile, outside), each,
        )
    for i in range(1, tile - 1):
        k.step(
            Plane(two, 1, i), first(1, i), Plane(f, 0, 2, i), Plane(coef, i),
            *near(lambda j: first(1, j), i, tile),
        )
    for i in range(1, tile - 1):

        def each(r, value, total, out, i=i):
            k.put(inside(i), r, k.get(inside(i), r) + two[1, i, r:r + k.n] * total)

        k.step(
            Plane(three, i), Plane(two, 0, i), first(0, i), Plane(coef, i),
            *near(lambda j: Plane(two, 0, j), i, tile), each,
        )
    rows = (tile - 2) * ny
    acc1[rows:] = jnp.broadcast_to(w[0:1], (acc1.shape[0] - rows, nz))
    for i in edge:
        for r in k.blocks():
            k.put(Plane(two, 1, i), r, jnp.zeros((k.n, nz), F32))


def outer_kernel(w, f, coef, one, ends, two, halo, rim, be, bo, acc2, wtwo, uthree, beyond, d):
    tile, ny, nz = coef.shape
    k = Work(w, ny, nz)
    edge = (0, tile - 1)
    for s, i in enumerate(edge):
        for r in k.blocks():
            k.put(Plane(d, s), r, halo[s, 0, r:r + k.n] * f[0, 0, i, r:r + k.n])
    for r in k.blocks():
        u2, w1 = k.unpack(be, bo, 0, r), k.unpack(be, bo, 1, r)
        for s, i in enumerate(edge):
            h = halo[s, 0, r:r + k.n]
            dv, total = k.flat(Plane(d, s), r)
            total = total + ends[0, s, r:r + k.n]
            k.put(Plane(beyond, s, 0), r, u2[s] + (1.0 + k.a) * dv + h * total)
            k.put(Plane(beyond, s, 1), r, w1[s] + h * f[0, 2, i, r:r + k.n])

    def first(n, i):
        return Plane(ends, n, edge.index(i)) if i in edge else Plane(one, n, i)

    for s, i in enumerate(edge):
        k.step(
            Plane(wtwo, s), first(1, i), Plane(f, 0, 2, i), Plane(coef, i),
            *near(lambda j: first(1, j), i, tile, (Plane(beyond, 0, 1), Plane(beyond, 1, 1))),
        )

        def each(r, value, total, out, s=s):
            k.put(
                Plane(acc2, base=s * ny), r,
                rim[s, r:r + k.n] + wtwo[s, r:r + k.n] * total,
            )

        k.step(
            Plane(uthree, s), Plane(two, 0, i), first(0, i), Plane(coef, i),
            *near(lambda j: Plane(two, 0, j), i, tile, (Plane(beyond, 0, 0), Plane(beyond, 1, 0))),
            each,
        )


def early_u_kernel(two, three, pe, po):
    _, tile, ny, nz = two.shape
    k = Work(None, ny, nz)

    def planes(i, j):
        return [Plane(two, 0, i), Plane(three, i), Plane(three, j), Plane(two, 1, i)]

    k.pack(pe, po, planes(1, 2), planes(tile - 2, tile - 3))


def early_w_kernel(w, coef, one, two, wtwo, pe, po, winner):
    tile, ny, nz = coef.shape
    k = Work(w, ny, nz)
    edge = (0, tile - 1)

    def second(i):
        return Plane(wtwo, edge.index(i)) if i in edge else Plane(two, 1, i)

    for i in range(1, tile - 1):
        k.step(
            Plane(winner, i - 1), second(i), Plane(one, 1, i), Plane(coef, i),
            *near(second, i, tile),
        )

    def planes(s, i, j):
        return [Plane(wtwo, s), Plane(winner, i - 1), Plane(winner, j - 1)]

    k.pack(pe, po, planes(0, 1, 2), planes(1, tile - 2, tile - 3))


def pick_kernel(be, bo, out):
    out[0], out[1] = be[2], bo[2]


def penalty_kernel(v, c, be, bo, other, pen, logs, rims):
    tile, ny, nz = v.shape
    k = Work(None, ny, nz)
    edge = (0, tile - 1)
    for i in range(tile):
        for r in k.blocks():
            k.put(Plane(logs, i + 1), r, jnp.log(c[i, r:r + k.n]))
    for r in k.blocks():
        mine = k.unpack(be, bo, 2, r)
        theirs = k.unpack(other.at[0:1], other.at[1:2], 0, r)
        for s, i in enumerate(edge):
            vel = jnp.where(k.first_core, mine[s], theirs[s])
            con = jnp.where(k.first_core, theirs[s], mine[s])
            con = jnp.where(k.has[s], con, 1.0)
            k.put(Plane(rims, s), r, jnp.where(k.has[s], vel, v[i, r:r + k.n]))
            k.put(
                Plane(logs, (0, tile + 1)[s]), r,
                jnp.where(k.has[s], jnp.log(con), logs[i + 1, r:r + k.n]),
            )
    for i in range(tile):
        below, above = near(lambda j: Plane(v, j), i, tile, (Plane(rims, 0), Plane(rims, 1)))
        for r in k.blocks():
            vx = (k.get(above, r) - k.get(below, r)) * 0.5
            lx = (logs[i + 2, r:r + k.n] - logs[i, r:r + k.n]) * 0.5
            _, up, down, left, right = k.shifts(Plane(v, i), r, True)
            vy, vz = (down - up) * 0.5, (right - left) * 0.5
            _, up, down, left, right = k.shifts(Plane(logs, i + 1), r, True)
            ly, lz = (down - up) * 0.5, (right - left) * 0.5
            ca = vy * lz - vz * ly
            cb = vz * lx - vx * lz
            cc = vx * ly - vy * lx
            k.put(Plane(pen, i), r, penalty_gain * (ca * ca + cb * cb + cc * cc))


def weigh_kernel(acc1, acc2, far1, far2, out):
    _, tile, ny, nz = out.shape
    k = Work(None, ny, nz)
    rows = (tile - 2) * ny
    labels = [jnp.broadcast_to(ref[rows:rows + 1], (k.n, nz)) for ref in (acc1, far1)]
    for i in range(tile):
        for r in k.blocks():
            if i in (0, tile - 1):
                at = (0 if i == 0 else ny) + r
                mine, other = acc2[at:at + k.n], far2[at:at + k.n]
            else:
                at = (i - 1) * ny + r
                mine, other = acc1[at:at + k.n], far1[at:at + k.n]
            k.put(Plane(out, 0, i), r, labels[0] * mine + labels[1] * other)
            k.put(Plane(out, 1, i), r, (1.0 - labels[0]) * mine + (1.0 - labels[1]) * other)


def renew(scale, value, part, rest, pen):
    return value * jnp.exp(-step_size * jnp.tanh(scale * (part + rest) + pen))


def renew_kernel(scale, w, part, rest, pen, v, c, coef, e, o):
    tile, ny, nz = v.shape
    k = Work(w, ny, nz)
    sound = k.a == 1.0
    for i in range(tile):
        for r in k.blocks():
            at = slice(r, r + k.n)
            new = renew(
                scale,
                jnp.where(sound, v[i, at], c[i, at]),
                jnp.where(sound, part[0, i, at], part[1, i, at]),
                jnp.where(sound, rest[0, i, at], rest[1, i, at]),
                pen[i, at],
            )
            k.put(
                Plane(coef, i), r,
                jnp.where(sound, speed_gain * new**2, diffuse_gain / new),
            )
    k.pack(e, o, [Plane(coef, 0), Plane(coef, 1)], [Plane(coef, tile - 2), Plane(coef, tile - 1)])


def models_kernel(scale, part, rest, pen, v, c, out):
    tile, ny, nz = v.shape
    k = Work(None, ny, nz)
    for n, ref in enumerate((v, c)):
        for i in range(tile):
            for r in k.blocks():
                at = slice(r, r + k.n)
                out[n, i, at] = renew(scale, ref[i, at], part[n, i, at], rest[n, i, at], pen[i, at])


def before_kernel(
    w, coef, old, ends, two, wtwo, three, uthree, winner, halo, beyond, ue, uo, we, wo,
    four, five, ring, lap, side, wthree, wide, prev, last,
):
    tile, ny, nz = coef.shape
    k = Work(w, ny, nz)
    edge = (0, tile - 1)
    for r in k.blocks():
        for s, value in enumerate(k.unpack(we, wo, 0, r)):
            k.put(Plane(last, s), r, value)
    for n in range(2):
        far = (((ue, uo, 0), (ue, uo, 1), (ue, uo, 2)), ((ue, uo, 3), (we, wo, 1), (we, wo, 2)))[n]
        for r in k.blocks():
            at = slice(r, r + k.n)
            two_far, three_far, three_end = (k.unpack(*block, r) for block in far)
            for s in range(2):
                wide[(1, tile + 4)[s], at] = three_far[s]
                wide[(0, tile + 5)[s], at] = three_end[s]
                prev[s, at] = two_far[s]

        def second(i):
            return Plane(wtwo, edge.index(i)) if n and i in edge else Plane(two, n, i)

        for s, i in enumerate(edge):
            known = Plane(last, s) if n else Plane(beyond, s, 0)
            earlier = Plane(beyond, s, 1) if n else Plane(halo, s, 1)
            k.step(
                Plane(side, n, s), known, earlier, Plane(halo, s, 0), second(i), Plane(prev, s),
            )
            if n:
                k.step(
                    Plane(wthree, s), second(i), Plane(ends, 1, s), Plane(old, i),
                    *near(second, i, tile, (Plane(last, 0), Plane(last, 1))),
                )
            for r in k.blocks():
                k.put(Plane(wide, (2, tile + 3)[s]), r, side[n, s, r:r + k.n])

        def third_plane(i):
            if i in edge:
                return Plane(wthree if n else uthree, edge.index(i))
            return Plane(winner, i - 1) if n else Plane(three, i)

        for i in range(tile):
            for r in k.blocks():
                k.put(Plane(wide, i + 3), r, k.get(third_plane(i), r))

        for i in range(tile):
            k.step(
                Plane(four, n, i), Plane(wide, i + 3), second(i), Plane(coef, i),
                Plane(wide, i + 2), Plane(wide, i + 4),
            )
        for s in range(2):
            for m, j in enumerate(((-2, -1), (tile + 1, tile))[s]):
                known = Plane(last, s) if n else Plane(beyond, s, 0)
                earlier = known if m else Plane(prev, s)
                for r in k.blocks():
                    value, total = k.lap(Plane(wide, j + 3), Plane(wide, j + 2), Plane(wide, j + 4), r)
                    k.put(Plane(ring, n, s, m), r, k.ahead(value, k.get(earlier, r)))
                    k.put(Plane(lap, n, s, m), r, total)
        for i in range(1, tile - 1):
            k.step(
                Plane(five, n, i - 1), Plane(four, n, i), third_plane(i), Plane(coef, i),
                Plane(four, n, i - 1), Plane(four, n, i + 1),
            )


def after_kernel(
    w, coef, four, five, ring, lap, side, uthree, wthree, e, o,
    out, cn, far, ends, res, sems,
):
    tile, ny, nz = coef.shape
    k = Work(w, ny, nz)
    edge = (0, tile - 1)
    for r in k.blocks():
        parts = [k.unpack(e, o, m, r) for m in range(2)]
        for s in range(2):
            order = (0, 1) if s == 0 else (1, 0)
            for m in range(2):
                k.put(Plane(cn, s, m), r, parts[order[m]][s])
    copies = []
    for n in range(2):
        for s in range(2):
            for m in range(2):
                for r in k.blocks():
                    at = slice(r, r + k.n)
                    far[s, m, at] = ring[n, s, m, at] + cn[s, m, at] * lap[n, s, m, at]
        for s, i in enumerate(edge):
            k.step(
                Plane(ends, s, 0), Plane(far, s, 1), Plane(side, n, s), Plane(cn, s, 1),
                Plane(far, s, 0), Plane(four, n, i),
            )
            k.step(
                Plane(ends, s, 1), Plane(four, n, i), Plane(wthree if n else uthree, s),
                Plane(coef, i),
                *near(lambda j: Plane(four, n, j), i, tile, (Plane(far, 0, 1), Plane(far, 1, 1))),
            )

        def fifth(i):
            return Plane(ends, edge.index(i), 1) if i in edge else Plane(five, n, i - 1)

        for i in range(tile):
            k.step(
                Plane(res, n, i), fifth(i), Plane(four, n, i), Plane(coef, i),
                *near(fifth, i, tile, (Plane(ends, 0, 0), Plane(ends, 1, 0))),
            )
            copies.append(pltpu.make_async_copy(res.at[n, i], out.at[0, n, i], sems.at[n, i]))
            copies[-1].start()
    for copy in copies:
        copy.wait()


def swap_pairs(even_block, odd_block):
    count = lax.axis_size("space")
    evens = [(i, i ^ 1) for i in range(count) if i ^ 1 < count]
    odds = [(i, ((i + 1) ^ 1) - 1) for i in range(count) if 0 <= ((i + 1) ^ 1) - 1 < count]
    odd_block = lax.ppermute(odd_block, "space", odds)
    even_block = lax.ppermute(even_block, "space", evens)
    return even_block, odd_block


def across(block, mask):
    count = lax.axis_size("src")
    return lax.ppermute(block, "src", [(i, i ^ mask) for i in range(count)])


def block_step(fields, velocity, conductivity, labels):
    tile, ny, nz = velocity.shape
    groups = lax.axis_size("src")
    assert tile >= 4 and labels.shape[0] == 1 and groups >= 4 and groups & (groups - 1) == 0
    scale = 1.0 / (20.0 * math.sqrt(groups))

    def planes(*lead):
        return (*lead, ny, nz)

    ae, ao, be, bo, coef, one, acc, w, fields, velocity, conductivity = call(
        isolated_kernel,
        [planes(4)] * 2 + [planes(3)] * 2 + [planes(tile), planes(2, tile), planes(tile)]
        + [(8, nz), fields.shape, velocity.shape, conductivity.shape],
        (
            labels,
            *(pltpu.with_memory_space_constraint(x, pltpu.HBM) for x in (fields, velocity, conductivity)),
        ),
        [planes(2)],
        [pl.BlockSpec(memory_space=pltpu.SMEM)] + [pl.BlockSpec(memory_space=pltpu.HBM)] * 3,
        [pltpu.SemaphoreType.DMA((3,))],
    )
    ae, ao = swap_pairs(ae, ao)
    be, bo = swap_pairs(be, bo)

    acc1, rim, ends, two, three, halo = call(
        inner_kernel,
        [((tile - 2) * ny + 8, nz), planes(2), planes(2, 2), planes(2, tile), planes(tile), planes(2, 2)],
        (w, fields, coef, one, acc, ae, ao),
        [planes(2)],
    )
    masks = [1 << k for k in reversed(range(groups.bit_length() - 1))]
    far1 = across(acc1, masks[0])
    ue, uo = call(early_u_kernel, [planes(4)] * 2, (two, three))
    ue, uo = swap_pairs(ue, uo)
    acc2, wtwo, uthree, beyond = call(
        outer_kernel,
        [(2 * ny, nz), planes(2), planes(2), planes(2, 2)],
        (w, fields, coef, one, ends, two, halo, rim, be, bo),
        [planes(2)],
    )
    far2 = across(acc2, masks[0])
    we, wo, winner = call(
        early_w_kernel, [planes(3), planes(3), planes(tile - 2)], (w, coef, one, two, wtwo)
    )
    we, wo = swap_pairs(we, wo)
    (other,) = call(pick_kernel, [planes(2)], (be, bo))
    other = across(other, 1)

    (part,) = call(weigh_kernel, [planes(2, tile)], (acc1, acc2, far1, far2))
    for mask in masks[1:-1]:
        part = part + across(part, mask)
    rest = across(part, masks[-1])
    (pen,) = call(
        penalty_kernel,
        [planes(tile)],
        (velocity, conductivity, be, bo, other),
        [planes(tile + 2), planes(2)],
    )
    coef_next, e, o = call(
        lambda *refs: renew_kernel(scale, *refs),
        [planes(tile), planes(2), planes(2)],
        (w, part, rest, pen, velocity, conductivity),
    )
    e, o = swap_pairs(e, o)
    (models,) = call(
        lambda *refs: models_kernel(scale, *refs),
        [planes(2, tile)], (part, rest, pen, velocity, conductivity),
    )
    four, five, ring, lap, side, wthree = call(
        before_kernel,
        [planes(2, tile), planes(2, tile - 2), planes(2, 2, 2), planes(2, 2, 2), planes(2, 2), planes(2)],
        (w, coef_next, coef, ends, two, wtwo, three, uthree, winner, halo, beyond, ue, uo, we, wo),
        [planes(tile + 6), planes(2), planes(2)],
    )
    (final,) = call(
        after_kernel,
        [planes(1, 2, tile)],
        (w, coef_next, four, five, ring, lap, side, uthree, wthree, e, o),
        [planes(2, 2), planes(2, 2), planes(2, 2), planes(2, tile)],
        None,
        [pltpu.SemaphoreType.DMA((2, tile))],
        pl.BlockSpec(memory_space=pltpu.HBM),
    )
    return final, models


def solution(mesh):
    in_specs = (
        P(("parts", "src"), None, "space", None, None),
        P(("parts", "space"), None, None),
        P(("parts", "space"), None, None),
        P(("parts", "src")),
    )
    out_specs = (
        P(("parts", "src"), None, "space", None, None),
        P(None, ("parts", "space"), None, None),
    )
    return jax.shard_map(
        block_step, mesh=mesh, in_specs=in_specs, out_specs=out_specs, check_vma=False
    )
```

```python
import math

import jax
import jax.numpy as jnp
from jax import lax
from jax.experimental import pallas as pl
from jax.experimental.pallas import tpu as pltpu
from jax.sharding import PartitionSpec as P


speed_gain = 0.25
diffuse_gain = 0.15
step_size = 0.1
penalty_gain = 50.0

VMEM = pl.BlockSpec(memory_space=pltpu.VMEM)
F32 = jnp.float32


def call(kernel, outs, args, scratch=(), specs=None, extra=(), out_spec=VMEM):
    size = sum(math.prod(o) for o in outs) + sum(a.size for a in args)
    return pl.pallas_call(
        kernel,
        out_shape=tuple(jax.ShapeDtypeStruct(o, F32) for o in outs),
        in_specs=specs or [VMEM for _ in args],
        out_specs=tuple(out_spec for _ in outs),
        scratch_shapes=[pltpu.VMEM(s, F32) for s in scratch] + list(extra),
        compiler_params=pltpu.CompilerParams(vmem_limit_bytes=16 << 20),
        cost_estimate=pl.CostEstimate(flops=20 * size, bytes_accessed=4 * size, transcendentals=0),
    )(*args)


class Plane:
    def __init__(self, ref, *at, base=0):
        self.ref, self.at, self.base = ref, at, base

    def _rows(self, r, n):
        return (*self.at, slice(self.base + r, self.base + r + n))

    def get(self, r, n):
        return self.ref[self._rows(r, n)]

    def put(self, r, n, value):
        self.ref[self._rows(r, n)] = value


class Work:
    def __init__(self, weight_ref, ny, nz):
        self.ny, self.n = ny, 32 if ny % 32 == 0 else ny
        shape = (self.n, nz)
        row = lax.broadcasted_iota(jnp.int32, shape, 0)
        col = lax.broadcasted_iota(jnp.int32, shape, 1)
        self.top, self.bottom = row == 0, row == self.n - 1
        self.left, self.right = col == 0, col == nz - 1
        self.nz = nz
        if weight_ref is not None:
            self.a = jnp.broadcast_to(weight_ref[0:1], shape)
        here = lax.axis_index("space")
        self.even = here % 2 == 0
        self.has = (here > 0, here < lax.axis_size("space") - 1)
        self.first_core = lax.axis_index("src") % 2 == 0

    def blocks(self):
        return range(0, self.ny, self.n)

    def get(self, plane, r):
        return plane.get(r, self.n)

    def put(self, plane, r, value):
        plane.put(r, self.n, value)

    def shifts(self, plane, r, edge):
        n, v = self.n, plane.get(r, self.n)

        def fill(test, moved):
            return jnp.where(test, v if edge else 0.0, moved)

        up = plane.get(r - 1, n) if r > 0 else fill(self.top, pltpu.roll(v, 1, 0))
        last = r + n == self.ny
        down = fill(self.bottom, pltpu.roll(v, n - 1, 0)) if last else plane.get(r + 1, n)
        left = fill(self.left, pltpu.roll(v, 1, 1))
        right = fill(self.right, pltpu.roll(v, self.nz - 1, 1))
        return v, up, down, left, right

    def flat(self, plane, r):
        v, up, down, left, right = self.shifts(plane, r, False)
        return v, ((up + down) + (left + right)) - 6.0 * v

    def lap(self, plane, below, above, r):
        v, total = self.flat(plane, r)
        for other in (below, above):
            if other is not None:
                total = total + self.get(other, r)
        return v, total

    def ahead(self, v, before):
        return (1.0 + self.a) * v - self.a * before

    def step(self, out, now, before, coef, below, above, each=None):
        for r in self.blocks():
            v, total = self.lap(now, below, above, r)
            value = self.ahead(v, self.get(before, r)) + self.get(coef, r) * total
            if out is not None:
                self.put(out, r, value)
            if each is not None:
                each(r, v, total, value)

    def coefficient(self, v, c):
        return self.a * speed_gain * v**2 + (1.0 - self.a) * diffuse_gain / c

    def pack(self, even_ref, odd_ref, lows, highs):
        for k, (low, high) in enumerate(zip(lows, highs)):
            for r in self.blocks():
                lo, hi = self.get(low, r), self.get(high, r)
                self.put(Plane(even_ref, k), r, jnp.where(self.even, hi, lo))
                self.put(Plane(odd_ref, k), r, jnp.where(self.even, lo, hi))

    def unpack(self, even_ref, odd_ref, k, r):
        e, o = self.get(Plane(even_ref, k), r), self.get(Plane(odd_ref, k), r)
        low, high = jnp.where(self.even, o, e), jnp.where(self.even, e, o)
        return jnp.where(self.has[0], low, 0.0), jnp.where(self.has[1], high, 0.0)


def near(make, i, tile, ends=(None, None)):
    return (make(i - 1) if i > 0 else ends[0]), (make(i + 1) if i < tile - 1 else ends[1])


def lead_kernel(label, f_in, v_in, c_in, ae, ao, coef, w, f, v, c, one, sems):
    parts = [(v_in, v), (c_in, c)] + [(f_in.at[0, n], f.at[0, n]) for n in (0, 1, 2, 3)]
    copies = [pltpu.make_async_copy(src, dst, sems.at[n]) for n, (src, dst) in enumerate(parts)]
    for copy in copies:
        copy.start()
    tile, ny, nz = v.shape
    w[...] = jnp.full(w.shape, label[0].astype(F32), F32)
    k = Work(w, ny, nz)
    edge = (0, tile - 1)
    copies[0].wait()
    copies[1].wait()
    for i in range(tile):
        for r in k.blocks():
            k.put(Plane(coef, i), r, k.coefficient(v[i, r:r + k.n], c[i, r:r + k.n]))
    copies[2].wait()
    copies[3].wait()
    for s, i in enumerate(edge):
        k.step(
            Plane(one, s), Plane(f, 0, 0, i), Plane(f, 0, 1, i), Plane(coef, i),
            *near(lambda j: Plane(f, 0, 0, j), i, tile),
        )
    copies[4].wait()
    k.pack(ae, ao, *(
        [Plane(coef, i), Plane(f, 0, 0, i), Plane(f, 0, 2, i), Plane(one, s)]
        for s, i in enumerate(edge)
    ))
    copies[5].wait()


def isolated_kernel(w, f, v, c, coef, be, bo, one, acc, two):
    tile, ny, nz = v.shape
    k = Work(w, ny, nz)
    edge = (0, tile - 1)
    for n in range(2):
        for i in range(tile):

            def each(r, value, total, out, i=i):
                k.put(Plane(acc, i), r, f[0, 2, i, r:r + k.n] * total)

            k.step(
                Plane(one, n, i), Plane(f, 0, 2 * n, i), Plane(f, 0, 2 * n + 1, i), Plane(coef, i),
                *near(lambda j: Plane(f, 0, 2 * n, j), i, tile), each if n == 0 else None,
            )
    for s, i in enumerate(edge):
        k.step(
            Plane(two, s), Plane(one, 0, i), Plane(f, 0, 0, i), Plane(coef, i),
            *near(lambda j: Plane(one, 0, j), i, tile),
        )
    k.pack(be, bo, *([Plane(two, s), Plane(one, 1, i)] for s, i in enumerate(edge)))
    for r in k.blocks():
        lo, hi = (
            jnp.where(k.first_core, v[i, r:r + k.n], c[i, r:r + k.n]) for i in edge
        )
        k.put(Plane(be, 2), r, jnp.where(k.even, hi, lo))
        k.put(Plane(bo, 2), r, jnp.where(k.even, lo, hi))


def inner_kernel(w, f, coef, one, acc, ae, ao, acc1, rim, ends, two, three, halo, zero):
    tile, ny, nz = coef.shape
    k = Work(w, ny, nz)
    edge = (0, tile - 1)
    for r in k.blocks():
        parts = [k.unpack(ae, ao, m, r) for m in range(4)]
        for s, i in enumerate(edge):
            h = [p[s] for p in parts]
            cf, w0, u0 = coef[i, r:r + k.n], f[0, 2, i, r:r + k.n], f[0, 0, i, r:r + k.n]
            k.put(Plane(halo, s, 0), r, h[0])
            k.put(Plane(halo, s, 1), r, h[3] + h[0] * u0)
            k.put(Plane(ends, 0, s), r, one[0, i, r:r + k.n] + cf * h[1])
            k.put(Plane(ends, 1, s), r, one[1, i, r:r + k.n] + cf * h[2])
            k.put(Plane(zero, s), r, acc[i, r:r + k.n] + w0 * h[1])

    def first(n, i):
        return Plane(ends, n, edge.index(i)) if i in edge else Plane(one, n, i)

    def inside(i):
        return Plane(acc1, base=(i - 1) * ny)

    outside = (Plane(halo, 0, 1), Plane(halo, 1, 1))
    for i in range(tile):

        def each(r, value, total, out, i=i):
            term = k.get(first(1, i), r) * total
            if i in edge:
                s = edge.index(i)
                k.put(Plane(rim, s), r, zero[s, r:r + k.n] + term)
            else:
                k.put(inside(i), r, acc[i, r:r + k.n] + term)

        k.step(
            Plane(two, 0, i), first(0, i), Plane(f, 0, 0, i), Plane(coef, i),
            *near(lambda j: first(0, j), i, tile, outside), each,
        )
    for i in range(1, tile - 1):
        k.step(
            Plane(two, 1, i), first(1, i), Plane(f, 0, 2, i), Plane(coef, i),
            *near(lambda j: first(1, j), i, tile),
        )
    for i in range(1, tile - 1):

        def each(r, value, total, out, i=i):
            k.put(inside(i), r, k.get(inside(i), r) + two[1, i, r:r + k.n] * total)

        k.step(
            Plane(three, i), Plane(two, 0, i), first(0, i), Plane(coef, i),
            *near(lambda j: Plane(two, 0, j), i, tile), each,
        )
    rows = (tile - 2) * ny
    acc1[rows:] = jnp.broadcast_to(w[0:1], (acc1.shape[0] - rows, nz))
    for i in edge:
        for r in k.blocks():
            k.put(Plane(two, 1, i), r, jnp.zeros((k.n, nz), F32))


def outer_kernel(w, f, coef, one, ends, two, halo, rim, be, bo, acc2, wtwo, uthree, beyond, d):
    tile, ny, nz = coef.shape
    k = Work(w, ny, nz)
    edge = (0, tile - 1)
    for s, i in enumerate(edge):
        for r in k.blocks():
            k.put(Plane(d, s), r, halo[s, 0, r:r + k.n] * f[0, 0, i, r:r + k.n])
    for r in k.blocks():
        u2, w1 = k.unpack(be, bo, 0, r), k.unpack(be, bo, 1, r)
        for s, i in enumerate(edge):
            h = halo[s, 0, r:r + k.n]
            dv, total = k.flat(Plane(d, s), r)
            total = total + ends[0, s, r:r + k.n]
            k.put(Plane(beyond, s, 0), r, u2[s] + (1.0 + k.a) * dv + h * total)
            k.put(Plane(beyond, s, 1), r, w1[s] + h * f[0, 2, i, r:r + k.n])

    def first(n, i):
        return Plane(ends, n, edge.index(i)) if i in edge else Plane(one, n, i)

    for s, i in enumerate(edge):
        k.step(
            Plane(wtwo, s), first(1, i), Plane(f, 0, 2, i), Plane(coef, i),
            *near(lambda j: first(1, j), i, tile, (Plane(beyond, 0, 1), Plane(beyond, 1, 1))),
        )

        def each(r, value, total, out, s=s):
            k.put(
                Plane(acc2, base=s * ny), r,
                rim[s, r:r + k.n] + wtwo[s, r:r + k.n] * total,
            )

        k.step(
            Plane(uthree, s), Plane(two, 0, i), first(0, i), Plane(coef, i),
            *near(lambda j: Plane(two, 0, j), i, tile, (Plane(beyond, 0, 0), Plane(beyond, 1, 0))),
            each,
        )


def early_u_kernel(two, three, pe, po):
    _, tile, ny, nz = two.shape
    k = Work(None, ny, nz)

    def planes(i, j):
        return [Plane(two, 0, i), Plane(three, i), Plane(three, j), Plane(two, 1, i)]

    k.pack(pe, po, planes(1, 2), planes(tile - 2, tile - 3))


def early_w_kernel(w, coef, one, two, wtwo, pe, po, winner):
    tile, ny, nz = coef.shape
    k = Work(w, ny, nz)
    edge = (0, tile - 1)

    def second(i):
        return Plane(wtwo, edge.index(i)) if i in edge else Plane(two, 1, i)

    for i in range(1, tile - 1):
        k.step(
            Plane(winner, i - 1), second(i), Plane(one, 1, i), Plane(coef, i),
            *near(second, i, tile),
        )

    def planes(s, i, j):
        return [Plane(wtwo, s), Plane(winner, i - 1), Plane(winner, j - 1)]

    k.pack(pe, po, planes(0, 1, 2), planes(1, tile - 2, tile - 3))


def pick_kernel(be, bo, out):
    out[0], out[1] = be[2], bo[2]


def penalty_kernel(v, c, be, bo, other, pen, logs, rims):
    tile, ny, nz = v.shape
    k = Work(None, ny, nz)
    edge = (0, tile - 1)
    for i in range(tile):
        for r in k.blocks():
            k.put(Plane(logs, i + 1), r, jnp.log(c[i, r:r + k.n]))
    for r in k.blocks():
        mine = k.unpack(be, bo, 2, r)
        theirs = k.unpack(other.at[0:1], other.at[1:2], 0, r)
        for s, i in enumerate(edge):
            vel = jnp.where(k.first_core, mine[s], theirs[s])
            con = jnp.where(k.first_core, theirs[s], mine[s])
            con = jnp.where(k.has[s], con, 1.0)
            k.put(Plane(rims, s), r, jnp.where(k.has[s], vel, v[i, r:r + k.n]))
            k.put(
                Plane(logs, (0, tile + 1)[s]), r,
                jnp.where(k.has[s], jnp.log(con), logs[i + 1, r:r + k.n]),
            )
    for i in range(tile):
        below, above = near(lambda j: Plane(v, j), i, tile, (Plane(rims, 0), Plane(rims, 1)))
        for r in k.blocks():
            vx = (k.get(above, r) - k.get(below, r)) * 0.5
            lx = (logs[i + 2, r:r + k.n] - logs[i, r:r + k.n]) * 0.5
            _, up, down, left, right = k.shifts(Plane(v, i), r, True)
            vy, vz = (down - up) * 0.5, (right - left) * 0.5
            _, up, down, left, right = k.shifts(Plane(logs, i + 1), r, True)
            ly, lz = (down - up) * 0.5, (right - left) * 0.5
            ca = vy * lz - vz * ly
            cb = vz * lx - vx * lz
            cc = vx * ly - vy * lx
            k.put(Plane(pen, i), r, penalty_gain * (ca * ca + cb * cb + cc * cc))


def weigh_kernel(acc1, acc2, far1, far2, out):
    _, tile, ny, nz = out.shape
    k = Work(None, ny, nz)
    rows = (tile - 2) * ny
    labels = [jnp.broadcast_to(ref[rows:rows + 1], (k.n, nz)) for ref in (acc1, far1)]
    for i in range(tile):
        for r in k.blocks():
            if i in (0, tile - 1):
                at = (0 if i == 0 else ny) + r
                mine, other = acc2[at:at + k.n], far2[at:at + k.n]
            else:
                at = (i - 1) * ny + r
                mine, other = acc1[at:at + k.n], far1[at:at + k.n]
            k.put(Plane(out, 0, i), r, labels[0] * mine + labels[1] * other)
            k.put(Plane(out, 1, i), r, (1.0 - labels[0]) * mine + (1.0 - labels[1]) * other)


def renew(scale, value, part, rest, pen):
    return value * jnp.exp(-step_size * jnp.tanh(scale * (part + rest) + pen))


def renew_kernel(scale, w, part, rest, pen, v, c, coef, e, o):
    tile, ny, nz = v.shape
    k = Work(w, ny, nz)
    sound = k.a == 1.0
    for i in range(tile):
        for r in k.blocks():
            at = slice(r, r + k.n)
            new = renew(
                scale,
                jnp.where(sound, v[i, at], c[i, at]),
                jnp.where(sound, part[0, i, at], part[1, i, at]),
                jnp.where(sound, rest[0, i, at], rest[1, i, at]),
                pen[i, at],
            )
            k.put(
                Plane(coef, i), r,
                jnp.where(sound, speed_gain * new**2, diffuse_gain / new),
            )
    k.pack(e, o, [Plane(coef, 0), Plane(coef, 1)], [Plane(coef, tile - 2), Plane(coef, tile - 1)])


def models_kernel(scale, part, rest, pen, v, c, out):
    tile, ny, nz = v.shape
    k = Work(None, ny, nz)
    for n, ref in enumerate((v, c)):
        for i in range(tile):
            for r in k.blocks():
                at = slice(r, r + k.n)
                out[n, i, at] = renew(scale, ref[i, at], part[n, i, at], rest[n, i, at], pen[i, at])


def before_kernel(
    w, coef, old, ends, two, wtwo, three, uthree, winner, halo, beyond, ue, uo, we, wo,
    four, five, ring, lap, side, wthree, wide, prev, last,
):
    tile, ny, nz = coef.shape
    k = Work(w, ny, nz)
    edge = (0, tile - 1)
    for r in k.blocks():
        for s, value in enumerate(k.unpack(we, wo, 0, r)):
            k.put(Plane(last, s), r, value)
    for n in range(2):
        far = (((ue, uo, 0), (ue, uo, 1), (ue, uo, 2)), ((ue, uo, 3), (we, wo, 1), (we, wo, 2)))[n]
        for r in k.blocks():
            at = slice(r, r + k.n)
            two_far, three_far, three_end = (k.unpack(*block, r) for block in far)
            for s in range(2):
                wide[(1, tile + 4)[s], at] = three_far[s]
                wide[(0, tile + 5)[s], at] = three_end[s]
                prev[s, at] = two_far[s]

        def second(i):
            return Plane(wtwo, edge.index(i)) if n and i in edge else Plane(two, n, i)

        for s, i in enumerate(edge):
            known = Plane(last, s) if n else Plane(beyond, s, 0)
            earlier = Plane(beyond, s, 1) if n else Plane(halo, s, 1)
            k.step(
                Plane(side, n, s), known, earlier, Plane(halo, s, 0), second(i), Plane(prev, s),
            )
            if n:
                k.step(
                    Plane(wthree, s), second(i), Plane(ends, 1, s), Plane(old, i),
                    *near(second, i, tile, (Plane(last, 0), Plane(last, 1))),
                )
            for r in k.blocks():
                k.put(Plane(wide, (2, tile + 3)[s]), r, side[n, s, r:r + k.n])

        def third_plane(i):
            if i in edge:
                return Plane(wthree if n else uthree, edge.index(i))
            return Plane(winner, i - 1) if n else Plane(three, i)

        for i in range(tile):
            for r in k.blocks():
                k.put(Plane(wide, i + 3), r, k.get(third_plane(i), r))

        for i in range(tile):
            k.step(
                Plane(four, n, i), Plane(wide, i + 3), second(i), Plane(coef, i),
                Plane(wide, i + 2), Plane(wide, i + 4),
            )
        for s in range(2):
            for m, j in enumerate(((-2, -1), (tile + 1, tile))[s]):
                known = Plane(last, s) if n else Plane(beyond, s, 0)
                earlier = known if m else Plane(prev, s)
                for r in k.blocks():
                    value, total = k.lap(Plane(wide, j + 3), Plane(wide, j + 2), Plane(wide, j + 4), r)
                    k.put(Plane(ring, n, s, m), r, k.ahead(value, k.get(earlier, r)))
                    k.put(Plane(lap, n, s, m), r, total)
        for i in range(1, tile - 1):
            k.step(
                Plane(five, n, i - 1), Plane(four, n, i), third_plane(i), Plane(coef, i),
                Plane(four, n, i - 1), Plane(four, n, i + 1),
            )


def after_kernel(
    w, coef, four, five, ring, lap, side, uthree, wthree, e, o,
    out, cn, far, ends, res, sems,
):
    tile, ny, nz = coef.shape
    k = Work(w, ny, nz)
    edge = (0, tile - 1)
    for r in k.blocks():
        parts = [k.unpack(e, o, m, r) for m in range(2)]
        for s in range(2):
            order = (0, 1) if s == 0 else (1, 0)
            for m in range(2):
                k.put(Plane(cn, s, m), r, parts[order[m]][s])
    copies = []
    for n in range(2):
        for s in range(2):
            for m in range(2):
                for r in k.blocks():
                    at = slice(r, r + k.n)
                    far[s, m, at] = ring[n, s, m, at] + cn[s, m, at] * lap[n, s, m, at]
        for s, i in enumerate(edge):
            k.step(
                Plane(ends, s, 0), Plane(far, s, 1), Plane(side, n, s), Plane(cn, s, 1),
                Plane(far, s, 0), Plane(four, n, i),
            )
            k.step(
                Plane(ends, s, 1), Plane(four, n, i), Plane(wthree if n else uthree, s),
                Plane(coef, i),
                *near(lambda j: Plane(four, n, j), i, tile, (Plane(far, 0, 1), Plane(far, 1, 1))),
            )

        def fifth(i):
            return Plane(ends, edge.index(i), 1) if i in edge else Plane(five, n, i - 1)

        for i in range(tile):
            k.step(
                Plane(res, n, i), fifth(i), Plane(four, n, i), Plane(coef, i),
                *near(fifth, i, tile, (Plane(ends, 0, 0), Plane(ends, 1, 0))),
            )
            copies.append(pltpu.make_async_copy(res.at[n, i], out.at[0, n, i], sems.at[n, i]))
            copies[-1].start()
    for copy in copies:
        copy.wait()


def swap_pairs(even_block, odd_block):
    count, groups = lax.axis_size("space"), lax.axis_size("src")

    def swap(block, partner):
        pairs = []
        for g in range(groups):
            for i in range(count):
                j = partner(i)
                to = g * count + j if 0 <= j < count else (g ^ 1) * count + i
                pairs.append((g * count + i, to))
        return lax.ppermute(block, ("src", "space"), pairs)

    odd_block = swap(odd_block, lambda i: ((i + 1) ^ 1) - 1)
    even_block = swap(even_block, lambda i: i ^ 1)
    return even_block, odd_block


def across(block, mask):
    count = lax.axis_size("src")
    return lax.ppermute(block, "src", [(i, i ^ mask) for i in range(count)])


def block_step(fields, velocity, conductivity, labels):
    tile, ny, nz = velocity.shape
    groups = lax.axis_size("src")
    assert tile >= 4 and labels.shape[0] == 1 and groups >= 4 and groups & (groups - 1) == 0
    scale = 1.0 / (20.0 * math.sqrt(groups))

    def planes(*lead):
        return (*lead, ny, nz)

    ae, ao, coef, w, fields, velocity, conductivity = call(
        lead_kernel,
        [planes(4)] * 2 + [planes(tile), (8, nz), fields.shape, velocity.shape, conductivity.shape],
        (
            labels,
            *(pltpu.with_memory_space_constraint(x, pltpu.HBM) for x in (fields, velocity, conductivity)),
        ),
        [planes(2)],
        [pl.BlockSpec(memory_space=pltpu.SMEM)] + [pl.BlockSpec(memory_space=pltpu.HBM)] * 3,
        [pltpu.SemaphoreType.DMA((6,))],
    )
    ae, ao = swap_pairs(ae, ao)
    be, bo, one, acc = call(
        isolated_kernel,
        [planes(3), planes(3), planes(2, tile), planes(tile)],
        (w, fields, velocity, conductivity, coef),
        [planes(2)],
    )
    be, bo = swap_pairs(be, bo)

    acc1, rim, ends, two, three, halo = call(
        inner_kernel,
        [((tile - 2) * ny + 8, nz), planes(2), planes(2, 2), planes(2, tile), planes(tile), planes(2, 2)],
        (w, fields, coef, one, acc, ae, ao),
        [planes(2)],
    )
    masks = [1 << k for k in reversed(range(groups.bit_length() - 1))]
    far1 = across(acc1, masks[0])
    ue, uo = call(early_u_kernel, [planes(4)] * 2, (two, three))
    ue, uo = swap_pairs(ue, uo)
    acc2, wtwo, uthree, beyond = call(
        outer_kernel,
        [(2 * ny, nz), planes(2), planes(2), planes(2, 2)],
        (w, fields, coef, one, ends, two, halo, rim, be, bo),
        [planes(2)],
    )
    far2 = across(acc2, masks[0])
    we, wo, winner = call(
        early_w_kernel, [planes(3), planes(3), planes(tile - 2)], (w, coef, one, two, wtwo)
    )
    we, wo = swap_pairs(we, wo)
    (other,) = call(pick_kernel, [planes(2)], (be, bo))
    other = across(other, 1)

    (part,) = call(weigh_kernel, [planes(2, tile)], (acc1, acc2, far1, far2))
    for mask in masks[1:-1]:
        part = part + across(part, mask)
    rest = across(part, masks[-1])
    (pen,) = call(
        penalty_kernel,
        [planes(tile)],
        (velocity, conductivity, be, bo, other),
        [planes(tile + 2), planes(2)],
    )
    coef_next, e, o = call(
        lambda *refs: renew_kernel(scale, *refs),
        [planes(tile), planes(2), planes(2)],
        (w, part, rest, pen, velocity, conductivity),
    )
    e, o = swap_pairs(e, o)
    (models,) = call(
        lambda *refs: models_kernel(scale, *refs),
        [planes(2, tile)], (part, rest, pen, velocity, conductivity),
    )
    four, five, ring, lap, side, wthree = call(
        before_kernel,
        [planes(2, tile), planes(2, tile - 2), planes(2, 2, 2), planes(2, 2, 2), planes(2, 2), planes(2)],
        (w, coef_next, coef, ends, two, wtwo, three, uthree, winner, halo, beyond, ue, uo, we, wo),
        [planes(tile + 6), planes(2), planes(2)],
    )
    (final,) = call(
        after_kernel,
        [planes(1, 2, tile)],
        (w, coef_next, four, five, ring, lap, side, uthree, wthree, e, o),
        [planes(2, 2), planes(2, 2), planes(2, 2), planes(2, tile)],
        None,
        [pltpu.SemaphoreType.DMA((2, tile))],
        pl.BlockSpec(memory_space=pltpu.HBM),
    )
    return final, models


def solution(mesh):
    in_specs = (
        P(("parts", "src"), None, "space", None, None),
        P(("parts", "space"), None, None),
        P(("parts", "space"), None, None),
        P(("parts", "src")),
    )
    out_specs = (
        P(("parts", "src"), None, "space", None, None),
        P(None, ("parts", "space"), None, None),
    )
    return jax.shard_map(
        block_step, mesh=mesh, in_specs=in_specs, out_specs=out_specs, check_vma=False
    )
```

```python
import math

import jax
import jax.numpy as jnp
from jax import lax
from jax.experimental import pallas as pl
from jax.experimental.pallas import tpu as pltpu
from jax.sharding import PartitionSpec as P


speed_gain = 0.25
diffuse_gain = 0.15
step_size = 0.1
penalty_gain = 50.0

VMEM = pl.BlockSpec(memory_space=pltpu.VMEM)
F32 = jnp.float32


def call(kernel, outs, args, scratch=(), specs=None, extra=(), out_spec=VMEM):
    size = sum(math.prod(o) for o in outs) + sum(a.size for a in args)
    return pl.pallas_call(
        kernel,
        out_shape=tuple(jax.ShapeDtypeStruct(o, F32) for o in outs),
        in_specs=specs or [VMEM for _ in args],
        out_specs=tuple(out_spec for _ in outs),
        scratch_shapes=[pltpu.VMEM(s, F32) for s in scratch] + list(extra),
        compiler_params=pltpu.CompilerParams(vmem_limit_bytes=16 << 20),
        cost_estimate=pl.CostEstimate(flops=20 * size, bytes_accessed=4 * size, transcendentals=0),
    )(*args)


class Plane:
    def __init__(self, ref, *at, base=0):
        self.ref, self.at, self.base = ref, at, base

    def _rows(self, r, n):
        return (*self.at, slice(self.base + r, self.base + r + n))

    def get(self, r, n):
        return self.ref[self._rows(r, n)]

    def put(self, r, n, value):
        self.ref[self._rows(r, n)] = value


class Work:
    def __init__(self, weight_ref, ny, nz):
        self.ny, self.n = ny, 32 if ny % 32 == 0 else ny
        shape = (self.n, nz)
        row = lax.broadcasted_iota(jnp.int32, shape, 0)
        col = lax.broadcasted_iota(jnp.int32, shape, 1)
        self.top, self.bottom = row == 0, row == self.n - 1
        self.left, self.right = col == 0, col == nz - 1
        self.nz = nz
        if weight_ref is not None:
            self.a = jnp.broadcast_to(weight_ref[0:1], shape)
        here = lax.axis_index("space")
        self.even = here % 2 == 0
        self.has = (here > 0, here < lax.axis_size("space") - 1)
        self.first_core = lax.axis_index("src") % 2 == 0

    def blocks(self):
        return range(0, self.ny, self.n)

    def get(self, plane, r):
        return plane.get(r, self.n)

    def put(self, plane, r, value):
        plane.put(r, self.n, value)

    def shifts(self, plane, r, edge):
        n, v = self.n, plane.get(r, self.n)

        def fill(test, moved):
            return jnp.where(test, v if edge else 0.0, moved)

        up = plane.get(r - 1, n) if r > 0 else fill(self.top, pltpu.roll(v, 1, 0))
        last = r + n == self.ny
        down = fill(self.bottom, pltpu.roll(v, n - 1, 0)) if last else plane.get(r + 1, n)
        left = fill(self.left, pltpu.roll(v, 1, 1))
        right = fill(self.right, pltpu.roll(v, self.nz - 1, 1))
        return v, up, down, left, right

    def flat(self, plane, r):
        v, up, down, left, right = self.shifts(plane, r, False)
        return v, ((up + down) + (left + right)) - 6.0 * v

    def lap(self, plane, below, above, r):
        v, total = self.flat(plane, r)
        for other in (below, above):
            if other is not None:
                total = total + self.get(other, r)
        return v, total

    def ahead(self, v, before):
        return (1.0 + self.a) * v - self.a * before

    def step(self, out, now, before, coef, below, above, each=None):
        for r in self.blocks():
            v, total = self.lap(now, below, above, r)
            value = self.ahead(v, self.get(before, r)) + self.get(coef, r) * total
            if out is not None:
                self.put(out, r, value)
            if each is not None:
                each(r, v, total, value)

    def coefficient(self, v, c):
        return self.a * speed_gain * v**2 + (1.0 - self.a) * diffuse_gain / c

    def models_beside(self, even_ref, odd_ref, other, r):
        mine = self.unpack(even_ref, odd_ref, 0, r)
        theirs = self.unpack(other.at[0:1], other.at[1:2], 0, r)
        out = []
        for s in range(2):
            vel = jnp.where(self.first_core, mine[s], theirs[s])
            con = jnp.where(self.first_core, theirs[s], mine[s])
            out.append((jnp.where(self.has[s], vel, 1.0), jnp.where(self.has[s], con, 1.0)))
        return out

    def pack(self, even_ref, odd_ref, lows, highs):
        for k, (low, high) in enumerate(zip(lows, highs)):
            for r in self.blocks():
                lo, hi = self.get(low, r), self.get(high, r)
                self.put(Plane(even_ref, k), r, jnp.where(self.even, hi, lo))
                self.put(Plane(odd_ref, k), r, jnp.where(self.even, lo, hi))

    def unpack(self, even_ref, odd_ref, k, r):
        e, o = self.get(Plane(even_ref, k), r), self.get(Plane(odd_ref, k), r)
        low, high = jnp.where(self.even, o, e), jnp.where(self.even, e, o)
        return jnp.where(self.has[0], low, 0.0), jnp.where(self.has[1], high, 0.0)


def near(make, i, tile, ends=(None, None)):
    return (make(i - 1) if i > 0 else ends[0]), (make(i + 1) if i < tile - 1 else ends[1])


def fetch_kernel(f_in, v_in, c_in, even, odd, f, v, c, sems):
    parts = [(v_in, v), (c_in, c)] + [(f_in.at[0, n], f.at[0, n]) for n in range(4)]
    copies = [pltpu.make_async_copy(src, dst, sems.at[n]) for n, (src, dst) in enumerate(parts)]
    for copy in copies:
        copy.start()
    tile, ny, nz = v.shape
    k = Work(None, ny, nz)
    edge = (0, tile - 1)
    for copy in copies[:3]:
        copy.wait()
    for r in k.blocks():
        lo, hi = (
            jnp.where(k.first_core, v[i, r:r + k.n], c[i, r:r + k.n]) for i in edge
        )
        k.put(Plane(even, 0), r, jnp.where(k.even, hi, lo))
        k.put(Plane(odd, 0), r, jnp.where(k.even, lo, hi))
    k.pack(even.at[1:], odd.at[1:], *([Plane(f, 0, 0, i)] for i in edge))
    for copy in copies[3:]:
        copy.wait()


def lead_kernel(label, f, v, c, even, odd, coef, w, one):
    tile, ny, nz = v.shape
    w[...] = jnp.full(w.shape, label[0].astype(F32), F32)
    k = Work(w, ny, nz)
    edge = (0, tile - 1)
    for i in range(tile):
        for r in k.blocks():
            k.put(Plane(coef, i), r, k.coefficient(v[i, r:r + k.n], c[i, r:r + k.n]))
    for s, i in enumerate(edge):
        k.step(
            Plane(one, s), Plane(f, 0, 0, i), Plane(f, 0, 1, i), Plane(coef, i),
            *near(lambda j: Plane(f, 0, 0, j), i, tile),
        )
    k.pack(even, odd, *([Plane(f, 0, 2, i), Plane(one, s)] for s, i in enumerate(edge)))


def isolated_kernel(w, f, coef, be, bo, one, acc, two):
    tile, ny, nz = coef.shape
    k = Work(w, ny, nz)
    edge = (0, tile - 1)
    for n in range(2):
        for i in range(tile):

            def each(r, value, total, out, i=i):
                k.put(Plane(acc, i), r, f[0, 2, i, r:r + k.n] * total)

            k.step(
                Plane(one, n, i), Plane(f, 0, 2 * n, i), Plane(f, 0, 2 * n + 1, i), Plane(coef, i),
                *near(lambda j: Plane(f, 0, 2 * n, j), i, tile), each if n == 0 else None,
            )
    for s, i in enumerate(edge):
        k.step(
            Plane(two, s), Plane(one, 0, i), Plane(f, 0, 0, i), Plane(coef, i),
            *near(lambda j: Plane(one, 0, j), i, tile),
        )
    k.pack(be, bo, *([Plane(two, s), Plane(one, 1, i)] for s, i in enumerate(edge)))


def inner_kernel(
    w, f, coef, one, acc, ae, ao, de, do, other, acc1, rim, ends, two, three, halo, zero,
):
    tile, ny, nz = coef.shape
    k = Work(w, ny, nz)
    edge = (0, tile - 1)
    for r in k.blocks():
        models = k.models_beside(ae, ao, other, r)
        parts = [k.unpack(ae, ao, 1, r)] + [k.unpack(de, do, m, r) for m in range(2)]
        for s, i in enumerate(edge):
            h = [jnp.where(k.has[s], k.coefficient(*models[s]), 0.0)] + [p[s] for p in parts]
            cf, w0, u0 = coef[i, r:r + k.n], f[0, 2, i, r:r + k.n], f[0, 0, i, r:r + k.n]
            k.put(Plane(halo, s, 0), r, h[0])
            k.put(Plane(halo, s, 1), r, h[3] + h[0] * u0)
            k.put(Plane(ends, 0, s), r, one[0, i, r:r + k.n] + cf * h[1])
            k.put(Plane(ends, 1, s), r, one[1, i, r:r + k.n] + cf * h[2])
            k.put(Plane(zero, s), r, acc[i, r:r + k.n] + w0 * h[1])

    def first(n, i):
        return Plane(ends, n, edge.index(i)) if i in edge else Plane(one, n, i)

    def inside(i):
        return Plane(acc1, base=(i - 1) * ny)

    outside = (Plane(halo, 0, 1), Plane(halo, 1, 1))
    for i in range(tile):

        def each(r, value, total, out, i=i):
            term = k.get(first(1, i), r) * total
            if i in edge:
                s = edge.index(i)
                k.put(Plane(rim, s), r, zero[s, r:r + k.n] + term)
            else:
                k.put(inside(i), r, acc[i, r:r + k.n] + term)

        k.step(
            Plane(two, 0, i), first(0, i), Plane(f, 0, 0, i), Plane(coef, i),
            *near(lambda j: first(0, j), i, tile, outside), each,
        )
    for i in range(1, tile - 1):
        k.step(
            Plane(two, 1, i), first(1, i), Plane(f, 0, 2, i), Plane(coef, i),
            *near(lambda j: first(1, j), i, tile),
        )
    for i in range(1, tile - 1):

        def each(r, value, total, out, i=i):
            k.put(inside(i), r, k.get(inside(i), r) + two[1, i, r:r + k.n] * total)

        k.step(
            Plane(three, i), Plane(two, 0, i), first(0, i), Plane(coef, i),
            *near(lambda j: Plane(two, 0, j), i, tile), each,
        )
    rows = (tile - 2) * ny
    acc1[rows:] = jnp.broadcast_to(w[0:1], (acc1.shape[0] - rows, nz))
    for i in edge:
        for r in k.blocks():
            k.put(Plane(two, 1, i), r, jnp.zeros((k.n, nz), F32))


def outer_kernel(w, f, coef, one, ends, two, halo, rim, be, bo, acc2, wtwo, uthree, beyond, d):
    tile, ny, nz = coef.shape
    k = Work(w, ny, nz)
    edge = (0, tile - 1)
    for s, i in enumerate(edge):
        for r in k.blocks():
            k.put(Plane(d, s), r, halo[s, 0, r:r + k.n] * f[0, 0, i, r:r + k.n])
    for r in k.blocks():
        u2, w1 = k.unpack(be, bo, 0, r), k.unpack(be, bo, 1, r)
        for s, i in enumerate(edge):
            h = halo[s, 0, r:r + k.n]
            dv, total = k.flat(Plane(d, s), r)
            total = total + ends[0, s, r:r + k.n]
            k.put(Plane(beyond, s, 0), r, u2[s] + (1.0 + k.a) * dv + h * total)
            k.put(Plane(beyond, s, 1), r, w1[s] + h * f[0, 2, i, r:r + k.n])

    def first(n, i):
        return Plane(ends, n, edge.index(i)) if i in edge else Plane(one, n, i)

    for s, i in enumerate(edge):
        k.step(
            Plane(wtwo, s), first(1, i), Plane(f, 0, 2, i), Plane(coef, i),
            *near(lambda j: first(1, j), i, tile, (Plane(beyond, 0, 1), Plane(beyond, 1, 1))),
        )

        def each(r, value, total, out, s=s):
            k.put(
                Plane(acc2, base=s * ny), r,
                rim[s, r:r + k.n] + wtwo[s, r:r + k.n] * total,
            )

        k.step(
            Plane(uthree, s), Plane(two, 0, i), first(0, i), Plane(coef, i),
            *near(lambda j: Plane(two, 0, j), i, tile, (Plane(beyond, 0, 0), Plane(beyond, 1, 0))),
            each,
        )


def early_u_kernel(two, three, pe, po):
    _, tile, ny, nz = two.shape
    k = Work(None, ny, nz)

    def planes(i, j):
        return [Plane(two, 0, i), Plane(three, i), Plane(three, j), Plane(two, 1, i)]

    k.pack(pe, po, planes(1, 2), planes(tile - 2, tile - 3))


def early_w_kernel(w, coef, one, two, wtwo, pe, po, winner):
    tile, ny, nz = coef.shape
    k = Work(w, ny, nz)
    edge = (0, tile - 1)

    def second(i):
        return Plane(wtwo, edge.index(i)) if i in edge else Plane(two, 1, i)

    for i in range(1, tile - 1):
        k.step(
            Plane(winner, i - 1), second(i), Plane(one, 1, i), Plane(coef, i),
            *near(second, i, tile),
        )

    def planes(s, i, j):
        return [Plane(wtwo, s), Plane(winner, i - 1), Plane(winner, j - 1)]

    k.pack(pe, po, planes(0, 1, 2), planes(1, tile - 2, tile - 3))


def pick_kernel(even, odd, out):
    out[0], out[1] = even[0], odd[0]


def penalty_kernel(v, c, ae, ao, other, pen, logs, rims):
    tile, ny, nz = v.shape
    k = Work(None, ny, nz)
    edge = (0, tile - 1)
    for i in range(tile):
        for r in k.blocks():
            k.put(Plane(logs, i + 1), r, jnp.log(c[i, r:r + k.n]))
    for r in k.blocks():
        models = k.models_beside(ae, ao, other, r)
        for s, i in enumerate(edge):
            vel, con = models[s]
            k.put(Plane(rims, s), r, jnp.where(k.has[s], vel, v[i, r:r + k.n]))
            k.put(
                Plane(logs, (0, tile + 1)[s]), r,
                jnp.where(k.has[s], jnp.log(con), logs[i + 1, r:r + k.n]),
            )
    for i in range(tile):
        below, above = near(lambda j: Plane(v, j), i, tile, (Plane(rims, 0), Plane(rims, 1)))
        for r in k.blocks():
            vx = (k.get(above, r) - k.get(below, r)) * 0.5
            lx = (logs[i + 2, r:r + k.n] - logs[i, r:r + k.n]) * 0.5
            _, up, down, left, right = k.shifts(Plane(v, i), r, True)
            vy, vz = (down - up) * 0.5, (right - left) * 0.5
            _, up, down, left, right = k.shifts(Plane(logs, i + 1), r, True)
            ly, lz = (down - up) * 0.5, (right - left) * 0.5
            ca = vy * lz - vz * ly
            cb = vz * lx - vx * lz
            cc = vx * ly - vy * lx
            k.put(Plane(pen, i), r, penalty_gain * (ca * ca + cb * cb + cc * cc))


def weigh_kernel(labels, far_labels, mine, other, out):
    _, planes, ny, nz = out.shape
    k = Work(None, ny, nz)
    last = labels.shape[0] - 8
    one, two = (jnp.broadcast_to(ref[last:last + 1], (k.n, nz)) for ref in (labels, far_labels))
    for i in range(planes):
        for r in k.blocks():
            at = slice(i * ny + r, i * ny + r + k.n)
            k.put(Plane(out, 0, i), r, one * mine[at] + two * other[at])
            k.put(Plane(out, 1, i), r, (1.0 - one) * mine[at] + (1.0 - two) * other[at])


def renew(scale, value, gradient, pen):
    return value * jnp.exp(-step_size * jnp.tanh(scale * gradient + pen))


class Sums:
    def __init__(self, part, rest, part_edge, rest_edge):
        self.inner, self.edge = (part, rest), (part_edge, rest_edge)
        self.tile = part.shape[1] + 2

    def get(self, n, i, at):
        edges = (0, self.tile - 1)
        pair, j = (self.edge, edges.index(i)) if i in edges else (self.inner, i - 1)
        return pair[0][n, j, at] + pair[1][n, j, at]


def renew_kernel(scale, w, part, rest, part_edge, rest_edge, pen, v, c, coef, e, o):
    tile, ny, nz = v.shape
    k = Work(w, ny, nz)
    sums = Sums(part, rest, part_edge, rest_edge)
    sound = k.a == 1.0
    for i in range(tile):
        for r in k.blocks():
            at = slice(r, r + k.n)
            new = renew(
                scale,
                jnp.where(sound, v[i, at], c[i, at]),
                jnp.where(sound, sums.get(0, i, at), sums.get(1, i, at)),
                pen[i, at],
            )
            k.put(
                Plane(coef, i), r,
                jnp.where(sound, speed_gain * new**2, diffuse_gain / new),
            )
    k.pack(e, o, [Plane(coef, 0), Plane(coef, 1)], [Plane(coef, tile - 2), Plane(coef, tile - 1)])


def models_kernel(scale, part, rest, part_edge, rest_edge, pen, v, c, out):
    tile, ny, nz = v.shape
    k = Work(None, ny, nz)
    sums = Sums(part, rest, part_edge, rest_edge)
    for n, ref in enumerate((v, c)):
        for i in range(tile):
            for r in k.blocks():
                at = slice(r, r + k.n)
                out[n, i, at] = renew(scale, ref[i, at], sums.get(n, i, at), pen[i, at])


def before_kernel(
    w, coef, old, ends, two, wtwo, three, uthree, winner, halo, beyond, ue, uo, we, wo,
    rim, six, ring, lap, side, wide, prev, last, wthree, four, five,
):
    tile, ny, nz = coef.shape
    k = Work(w, ny, nz)
    edge = (0, tile - 1)
    for r in k.blocks():
        for s, value in enumerate(k.unpack(we, wo, 0, r)):
            k.put(Plane(last, s), r, value)
    for n in range(2):
        far = (((ue, uo, 0), (ue, uo, 1), (ue, uo, 2)), ((ue, uo, 3), (we, wo, 1), (we, wo, 2)))[n]
        for r in k.blocks():
            at = slice(r, r + k.n)
            two_far, three_far, three_end = (k.unpack(*block, r) for block in far)
            for s in range(2):
                wide[(1, tile + 4)[s], at] = three_far[s]
                wide[(0, tile + 5)[s], at] = three_end[s]
                prev[s, at] = two_far[s]

        def second(i):
            return Plane(wtwo, edge.index(i)) if n and i in edge else Plane(two, n, i)

        for s, i in enumerate(edge):
            known = Plane(last, s) if n else Plane(beyond, s, 0)
            earlier = Plane(beyond, s, 1) if n else Plane(halo, s, 1)
            k.step(
                Plane(side, n, s), known, earlier, Plane(halo, s, 0), second(i), Plane(prev, s),
            )
            if n:
                k.step(
                    Plane(wthree, s), second(i), Plane(ends, 1, s), Plane(old, i),
                    *near(second, i, tile, (Plane(last, 0), Plane(last, 1))),
                )
            for r in k.blocks():
                k.put(Plane(wide, (2, tile + 3)[s]), r, side[n, s, r:r + k.n])

        def third_plane(i):
            if i in edge:
                return Plane(wthree if n else uthree, edge.index(i))
            return Plane(winner, i - 1) if n else Plane(three, i)

        for i in range(tile):
            for r in k.blocks():
                k.put(Plane(wide, i + 3), r, k.get(third_plane(i), r))

        for i in range(tile):
            k.step(
                Plane(four, i), Plane(wide, i + 3), second(i), Plane(coef, i),
                Plane(wide, i + 2), Plane(wide, i + 4),
            )
        for s in range(2):
            for m, j in enumerate(((-2, -1), (tile + 1, tile))[s]):
                known = Plane(last, s) if n else Plane(beyond, s, 0)
                earlier = known if m else Plane(prev, s)
                for r in k.blocks():
                    value, total = k.lap(Plane(wide, j + 3), Plane(wide, j + 2), Plane(wide, j + 4), r)
                    k.put(Plane(ring, n, s, m), r, k.ahead(value, k.get(earlier, r)))
                    k.put(Plane(lap, n, s, m), r, total)
        for i in range(tile):
            k.step(
                Plane(five, i), Plane(four, i), third_plane(i), Plane(coef, i),
                *near(lambda j: Plane(four, j), i, tile),
            )
        for i in range(tile):
            k.step(
                Plane(six, n, i), Plane(five, i), Plane(four, i), Plane(coef, i),
                *near(lambda j: Plane(five, j), i, tile),
            )
        for s, i in enumerate(edge):
            for r in k.blocks():
                k.put(Plane(rim, n, s), r, k.get(Plane(four, i), r))


def after_kernel(w, coef, rim, six, ring, lap, side, e, o, out, res, close, away, d, h5, sems):
    _, tile, ny, nz = six.shape
    k = Work(w, ny, nz)
    edge, next_to = (0, tile - 1), (1, tile - 2)
    copies = []

    def send(n, i):
        copies.append(pltpu.make_async_copy(res.at[n, i], out.at[0, n, i], sems.at[n, i]))
        copies[-1].start()

    for n in range(2):
        for i in range(2, tile - 2):
            for r in k.blocks():
                k.put(Plane(res, n, i), r, k.get(Plane(six, n, i), r))
            send(n, i)
        for s, i in enumerate(edge):
            for r in k.blocks():
                at = slice(r, r + k.n)
                outer, inner = (k.unpack(e, o, (m, 1 - m)[s], r)[s] for m in range(2))
                near_plane = ring[n, s, 1, at] + inner * lap[n, s, 1, at]
                close[n, s, at] = near_plane
                away[n, s, at] = (
                    k.ahead(near_plane, side[n, s, at])
                    + inner * (ring[n, s, 0, at] + outer * lap[n, s, 0, at] + rim[n, s, at])
                )
                h5[n, s, at] = inner
                delta = coef[i, at] * near_plane
                d[n, s, at] = delta
                j = next_to[s]
                res[n, j, at] = six[n, j, at] + coef[j, at] * delta
            send(n, next_to[s])
        for s, i in enumerate(edge):
            for r in k.blocks():
                at = slice(r, r + k.n)
                _, total = k.flat(Plane(close, n, s), r)
                fifth = away[n, s, at] + h5[n, s, at] * total
                delta, total = k.flat(Plane(d, n, s), r)
                res[n, i, at] = (
                    six[n, i, at] + (1.0 + k.a) * delta + coef[i, at] * (total + fifth)
                )
            send(n, i)
    for copy in copies:
        copy.wait()


def swap_pairs(even_block, odd_block):
    count, groups = lax.axis_size("space"), lax.axis_size("src")

    def swap(block, partner):
        pairs = []
        for g in range(groups):
            for i in range(count):
                j = partner(i)
                to = g * count + j if 0 <= j < count else (g ^ 1) * count + i
                pairs.append((g * count + i, to))
        return lax.ppermute(block, ("src", "space"), pairs)

    odd_block = swap(odd_block, lambda i: ((i + 1) ^ 1) - 1)
    even_block = swap(even_block, lambda i: i ^ 1)
    return even_block, odd_block


def across(block, mask):
    count = lax.axis_size("src")
    return lax.ppermute(block, "src", [(i, i ^ mask) for i in range(count)])


def block_step(fields, velocity, conductivity, labels):
    tile, ny, nz = velocity.shape
    groups = lax.axis_size("src")
    assert tile >= 4 and labels.shape[0] == 1 and groups >= 4 and groups & (groups - 1) == 0
    scale = 1.0 / (20.0 * math.sqrt(groups))

    def planes(*lead):
        return (*lead, ny, nz)

    ae, ao, fields, velocity, conductivity = call(
        fetch_kernel,
        [planes(2)] * 2 + [fields.shape, velocity.shape, conductivity.shape],
        tuple(pltpu.with_memory_space_constraint(x, pltpu.HBM) for x in (fields, velocity, conductivity)),
        (),
        [pl.BlockSpec(memory_space=pltpu.HBM)] * 3,
        [pltpu.SemaphoreType.DMA((6,))],
    )
    ae, ao = swap_pairs(ae, ao)
    de, do, coef, w = call(
        lead_kernel,
        [planes(2)] * 2 + [planes(tile), (8, nz)],
        (labels, fields, velocity, conductivity),
        [planes(2)],
        [pl.BlockSpec(memory_space=pltpu.SMEM)] + [VMEM] * 3,
    )
    de, do = swap_pairs(de, do)
    be, bo, one, acc = call(
        isolated_kernel,
        [planes(2)] * 2 + [planes(2, tile), planes(tile)],
        (w, fields, coef),
        [planes(2)],
    )
    be, bo = swap_pairs(be, bo)
    (other,) = call(pick_kernel, [planes(2)], (ae, ao))
    other = across(other, 1)

    acc1, rim, ends, two, three, halo = call(
        inner_kernel,
        [((tile - 2) * ny + 8, nz), planes(2), planes(2, 2), planes(2, tile), planes(tile), planes(2, 2)],
        (w, fields, coef, one, acc, ae, ao, de, do, other),
        [planes(2)],
    )
    masks = [1 << k for k in reversed(range(groups.bit_length() - 1))]
    far1 = across(acc1, masks[0])
    ue, uo = call(early_u_kernel, [planes(4)] * 2, (two, three))
    ue, uo = swap_pairs(ue, uo)
    acc2, wtwo, uthree, beyond = call(
        outer_kernel,
        [(2 * ny, nz), planes(2), planes(2), planes(2, 2)],
        (w, fields, coef, one, ends, two, halo, rim, be, bo),
        [planes(2)],
    )
    far2 = across(acc2, masks[0])
    we, wo, winner = call(
        early_w_kernel, [planes(3), planes(3), planes(tile - 2)], (w, coef, one, two, wtwo)
    )
    we, wo = swap_pairs(we, wo)
    (pen,) = call(
        penalty_kernel,
        [planes(tile)],
        (velocity, conductivity, ae, ao, other),
        [planes(tile + 2), planes(2)],
    )

    sums = []
    for mine, far in ((acc1, far1), (acc2, far2)):
        rows = mine.shape[0] // ny
        (part,) = call(weigh_kernel, [planes(2, rows)], (acc1, far1, mine, far))
        for mask in masks[1:-1]:
            part = part + across(part, mask)
        sums += [part, across(part, masks[-1])]
    coef_next, e, o = call(
        lambda *refs: renew_kernel(scale, *refs),
        [planes(tile), planes(2), planes(2)],
        (w, *sums, pen, velocity, conductivity),
    )
    e, o = swap_pairs(e, o)
    (models,) = call(
        lambda *refs: models_kernel(scale, *refs),
        [planes(2, tile)], (*sums, pen, velocity, conductivity),
    )
    rim, six, ring, lap, side = call(
        before_kernel,
        [planes(2, 2), planes(2, tile), planes(2, 2, 2), planes(2, 2, 2), planes(2, 2)],
        (w, coef_next, coef, ends, two, wtwo, three, uthree, winner, halo, beyond, ue, uo, we, wo),
        [planes(tile + 6), planes(2), planes(2), planes(2), planes(tile), planes(tile)],
    )
    (final,) = call(
        after_kernel,
        [planes(1, 2, tile)],
        (w, coef_next, rim, six, ring, lap, side, e, o),
        [planes(2, tile), planes(2, 2), planes(2, 2), planes(2, 2), planes(2, 2)],
        None,
        [pltpu.SemaphoreType.DMA((2, tile))],
        pl.BlockSpec(memory_space=pltpu.HBM),
    )
    return final, models


def solution(mesh):
    in_specs = (
        P(("parts", "src"), None, "space", None, None),
        P(("parts", "space"), None, None),
        P(("parts", "space"), None, None),
        P(("parts", "src")),
    )
    out_specs = (
        P(("parts", "src"), None, "space", None, None),
        P(None, ("parts", "space"), None, None),
    )
    return jax.shard_map(
        block_step, mesh=mesh, in_specs=in_specs, out_specs=out_specs, check_vma=False
    )
```

```python
import math

import jax
import jax.numpy as jnp
from jax import lax
from jax.experimental import pallas as pl
from jax.experimental.pallas import tpu as pltpu
from jax.sharding import PartitionSpec as P


speed_gain = 0.25
diffuse_gain = 0.15
step_size = 0.1
penalty_gain = 50.0

VMEM = pl.BlockSpec(memory_space=pltpu.VMEM)
F32 = jnp.float32


def call(kernel, outs, args, scratch=(), specs=None, extra=(), out_spec=VMEM):
    size = sum(math.prod(o) for o in outs) + sum(a.size for a in args)
    return pl.pallas_call(
        kernel,
        out_shape=tuple(jax.ShapeDtypeStruct(o, F32) for o in outs),
        in_specs=specs or [VMEM for _ in args],
        out_specs=tuple(out_spec for _ in outs),
        scratch_shapes=[pltpu.VMEM(s, F32) for s in scratch] + list(extra),
        compiler_params=pltpu.CompilerParams(vmem_limit_bytes=16 << 20),
        cost_estimate=pl.CostEstimate(flops=20 * size, bytes_accessed=4 * size, transcendentals=0),
    )(*args)


class Plane:
    def __init__(self, ref, *at, base=0):
        self.ref, self.at, self.base = ref, at, base

    def _rows(self, r, n):
        return (*self.at, slice(self.base + r, self.base + r + n))

    def get(self, r, n):
        return self.ref[self._rows(r, n)]

    def put(self, r, n, value):
        self.ref[self._rows(r, n)] = value


class Work:
    def __init__(self, weight_ref, ny, nz):
        self.ny, self.n = ny, 32 if ny % 32 == 0 else ny
        shape = (self.n, nz)
        row = lax.broadcasted_iota(jnp.int32, shape, 0)
        col = lax.broadcasted_iota(jnp.int32, shape, 1)
        self.top, self.bottom = row == 0, row == self.n - 1
        self.left, self.right = col == 0, col == nz - 1
        self.nz = nz
        if weight_ref is not None:
            self.a = jnp.broadcast_to(weight_ref[0:1], shape)
        here = lax.axis_index("space")
        self.even = here % 2 == 0
        self.has = (here > 0, here < lax.axis_size("space") - 1)
        self.first_core = lax.axis_index("src") % 2 == 0

    def blocks(self):
        return range(0, self.ny, self.n)

    def get(self, plane, r):
        return plane.get(r, self.n)

    def put(self, plane, r, value):
        plane.put(r, self.n, value)

    def shifts(self, plane, r, edge):
        n, v = self.n, plane.get(r, self.n)

        def fill(test, moved):
            return jnp.where(test, v if edge else 0.0, moved)

        up = plane.get(r - 1, n) if r > 0 else fill(self.top, pltpu.roll(v, 1, 0))
        last = r + n == self.ny
        down = fill(self.bottom, pltpu.roll(v, n - 1, 0)) if last else plane.get(r + 1, n)
        left = fill(self.left, pltpu.roll(v, 1, 1))
        right = fill(self.right, pltpu.roll(v, self.nz - 1, 1))
        return v, up, down, left, right

    def flat(self, plane, r):
        v, up, down, left, right = self.shifts(plane, r, False)
        return v, ((up + down) + (left + right)) - 6.0 * v

    def lap(self, plane, below, above, r):
        v, total = self.flat(plane, r)
        for other in (below, above):
            if other is not None:
                total = total + self.get(other, r)
        return v, total

    def ahead(self, v, before):
        return (1.0 + self.a) * v - self.a * before

    def step(self, out, now, before, coef, below, above, each=None):
        for r in self.blocks():
            v, total = self.lap(now, below, above, r)
            value = self.ahead(v, self.get(before, r)) + self.get(coef, r) * total
            if out is not None:
                self.put(out, r, value)
            if each is not None:
                each(r, v, total, value)

    def coefficient(self, v, c):
        return self.a * speed_gain * v**2 + (1.0 - self.a) * diffuse_gain / c

    def models_beside(self, even_ref, odd_ref, other, r):
        mine = self.unpack(even_ref, odd_ref, 0, r)
        theirs = self.unpack(other.at[0:1], other.at[1:2], 0, r)
        out = []
        for s in range(2):
            vel = jnp.where(self.first_core, mine[s], theirs[s])
            con = jnp.where(self.first_core, theirs[s], mine[s])
            out.append((jnp.where(self.has[s], vel, 1.0), jnp.where(self.has[s], con, 1.0)))
        return out

    def pack(self, even_ref, odd_ref, lows, highs):
        for k, (low, high) in enumerate(zip(lows, highs)):
            for r in self.blocks():
                lo, hi = self.get(low, r), self.get(high, r)
                self.put(Plane(even_ref, k), r, jnp.where(self.even, hi, lo))
                self.put(Plane(odd_ref, k), r, jnp.where(self.even, lo, hi))

    def unpack(self, even_ref, odd_ref, k, r):
        e, o = self.get(Plane(even_ref, k), r), self.get(Plane(odd_ref, k), r)
        low, high = jnp.where(self.even, o, e), jnp.where(self.even, e, o)
        return jnp.where(self.has[0], low, 0.0), jnp.where(self.has[1], high, 0.0)


def near(make, i, tile, ends=(None, None)):
    return (make(i - 1) if i > 0 else ends[0]), (make(i + 1) if i < tile - 1 else ends[1])


def fetch_kernel(f_in, v_in, c_in, even, odd, buf, sems):
    tile, ny, nz = v_in.shape
    k = Work(None, ny, nz)
    copies = []
    for n, src in enumerate((v_in, c_in, f_in.at[0, 0])):
        for s, i in enumerate((0, tile - 1)):
            copies.append(pltpu.make_async_copy(src.at[i], buf.at[n, s], sems.at[n, s]))
            copies[-1].start()
    for copy in copies:
        copy.wait()
    for r in k.blocks():
        at = slice(r, r + k.n)
        lo, hi = (jnp.where(k.first_core, buf[0, s, at], buf[1, s, at]) for s in range(2))
        k.put(Plane(even, 0), r, jnp.where(k.even, hi, lo))
        k.put(Plane(odd, 0), r, jnp.where(k.even, lo, hi))
    k.pack(even.at[1:], odd.at[1:], [Plane(buf, 2, 0)], [Plane(buf, 2, 1)])


def lead_kernel(label, f, v, c, even, odd, coef, w, one):
    tile, ny, nz = v.shape
    w[...] = jnp.full(w.shape, label[0].astype(F32), F32)
    k = Work(w, ny, nz)
    edge = (0, tile - 1)
    for i in range(tile):
        for r in k.blocks():
            k.put(Plane(coef, i), r, k.coefficient(v[i, r:r + k.n], c[i, r:r + k.n]))
    for s, i in enumerate(edge):
        k.step(
            Plane(one, s), Plane(f, 0, 0, i), Plane(f, 0, 1, i), Plane(coef, i),
            *near(lambda j: Plane(f, 0, 0, j), i, tile),
        )
    k.pack(even, odd, *([Plane(f, 0, 2, i), Plane(one, s)] for s, i in enumerate(edge)))


def isolated_kernel(w, f, coef, be, bo, one, acc, two):
    tile, ny, nz = coef.shape
    k = Work(w, ny, nz)
    edge = (0, tile - 1)
    for n in range(2):
        for i in range(tile):

            def each(r, value, total, out, i=i):
                k.put(Plane(acc, i), r, f[0, 2, i, r:r + k.n] * total)

            k.step(
                Plane(one, n, i), Plane(f, 0, 2 * n, i), Plane(f, 0, 2 * n + 1, i), Plane(coef, i),
                *near(lambda j: Plane(f, 0, 2 * n, j), i, tile), each if n == 0 else None,
            )
    for s, i in enumerate(edge):
        k.step(
            Plane(two, s), Plane(one, 0, i), Plane(f, 0, 0, i), Plane(coef, i),
            *near(lambda j: Plane(one, 0, j), i, tile),
        )
    k.pack(be, bo, *([Plane(two, s), Plane(one, 1, i)] for s, i in enumerate(edge)))


def inner_kernel(
    w, f, coef, one, acc, ae, ao, de, do, other, acc1, rim, ends, two, three, halo, zero,
):
    tile, ny, nz = coef.shape
    k = Work(w, ny, nz)
    edge = (0, tile - 1)
    for r in k.blocks():
        models = k.models_beside(ae, ao, other, r)
        parts = [k.unpack(ae, ao, 1, r)] + [k.unpack(de, do, m, r) for m in range(2)]
        for s, i in enumerate(edge):
            h = [jnp.where(k.has[s], k.coefficient(*models[s]), 0.0)] + [p[s] for p in parts]
            cf, w0, u0 = coef[i, r:r + k.n], f[0, 2, i, r:r + k.n], f[0, 0, i, r:r + k.n]
            k.put(Plane(halo, s, 0), r, h[0])
            k.put(Plane(halo, s, 1), r, h[3] + h[0] * u0)
            k.put(Plane(ends, 0, s), r, one[0, i, r:r + k.n] + cf * h[1])
            k.put(Plane(ends, 1, s), r, one[1, i, r:r + k.n] + cf * h[2])
            k.put(Plane(zero, s), r, acc[i, r:r + k.n] + w0 * h[1])

    def first(n, i):
        return Plane(ends, n, edge.index(i)) if i in edge else Plane(one, n, i)

    def inside(i):
        return Plane(acc1, base=(i - 1) * ny)

    outside = (Plane(halo, 0, 1), Plane(halo, 1, 1))
    for i in range(tile):

        def each(r, value, total, out, i=i):
            term = k.get(first(1, i), r) * total
            if i in edge:
                s = edge.index(i)
                k.put(Plane(rim, s), r, zero[s, r:r + k.n] + term)
            else:
                k.put(inside(i), r, acc[i, r:r + k.n] + term)

        k.step(
            Plane(two, 0, i), first(0, i), Plane(f, 0, 0, i), Plane(coef, i),
            *near(lambda j: first(0, j), i, tile, outside), each,
        )
    for i in range(1, tile - 1):
        k.step(
            Plane(two, 1, i), first(1, i), Plane(f, 0, 2, i), Plane(coef, i),
            *near(lambda j: first(1, j), i, tile),
        )
    for i in range(1, tile - 1):

        def each(r, value, total, out, i=i):
            k.put(inside(i), r, k.get(inside(i), r) + two[1, i, r:r + k.n] * total)

        k.step(
            Plane(three, i), Plane(two, 0, i), first(0, i), Plane(coef, i),
            *near(lambda j: Plane(two, 0, j), i, tile), each,
        )
    rows = (tile - 2) * ny
    acc1[rows:] = jnp.broadcast_to(w[0:1], (acc1.shape[0] - rows, nz))
    for i in edge:
        for r in k.blocks():
            k.put(Plane(two, 1, i), r, jnp.zeros((k.n, nz), F32))


def outer_kernel(w, f, coef, one, ends, two, halo, rim, be, bo, acc2, wtwo, uthree, beyond, d):
    tile, ny, nz = coef.shape
    k = Work(w, ny, nz)
    edge = (0, tile - 1)
    for s, i in enumerate(edge):
        for r in k.blocks():
            k.put(Plane(d, s), r, halo[s, 0, r:r + k.n] * f[0, 0, i, r:r + k.n])
    for r in k.blocks():
        u2, w1 = k.unpack(be, bo, 0, r), k.unpack(be, bo, 1, r)
        for s, i in enumerate(edge):
            h = halo[s, 0, r:r + k.n]
            dv, total = k.flat(Plane(d, s), r)
            total = total + ends[0, s, r:r + k.n]
            k.put(Plane(beyond, s, 0), r, u2[s] + (1.0 + k.a) * dv + h * total)
            k.put(Plane(beyond, s, 1), r, w1[s] + h * f[0, 2, i, r:r + k.n])

    def first(n, i):
        return Plane(ends, n, edge.index(i)) if i in edge else Plane(one, n, i)

    for s, i in enumerate(edge):
        k.step(
            Plane(wtwo, s), first(1, i), Plane(f, 0, 2, i), Plane(coef, i),
            *near(lambda j: first(1, j), i, tile, (Plane(beyond, 0, 1), Plane(beyond, 1, 1))),
        )

        def each(r, value, total, out, s=s):
            k.put(
                Plane(acc2, base=s * ny), r,
                rim[s, r:r + k.n] + wtwo[s, r:r + k.n] * total,
            )

        k.step(
            Plane(uthree, s), Plane(two, 0, i), first(0, i), Plane(coef, i),
            *near(lambda j: Plane(two, 0, j), i, tile, (Plane(beyond, 0, 0), Plane(beyond, 1, 0))),
            each,
        )


def early_u_kernel(two, three, pe, po):
    _, tile, ny, nz = two.shape
    k = Work(None, ny, nz)

    def planes(i, j):
        return [Plane(two, 0, i), Plane(three, i), Plane(three, j), Plane(two, 1, i)]

    k.pack(pe, po, planes(1, 2), planes(tile - 2, tile - 3))


def early_w_kernel(w, coef, one, two, wtwo, pe, po, winner):
    tile, ny, nz = coef.shape
    k = Work(w, ny, nz)
    edge = (0, tile - 1)

    def second(i):
        return Plane(wtwo, edge.index(i)) if i in edge else Plane(two, 1, i)

    for i in range(1, tile - 1):
        k.step(
            Plane(winner, i - 1), second(i), Plane(one, 1, i), Plane(coef, i),
            *near(second, i, tile),
        )

    def planes(s, i, j):
        return [Plane(wtwo, s), Plane(winner, i - 1), Plane(winner, j - 1)]

    k.pack(pe, po, planes(0, 1, 2), planes(1, tile - 2, tile - 3))


def pick_kernel(even, odd, out):
    out[0], out[1] = even[0], odd[0]


def penalty_kernel(v, c, ae, ao, other, pen, logs, rims):
    tile, ny, nz = v.shape
    k = Work(None, ny, nz)
    edge = (0, tile - 1)
    for i in range(tile):
        for r in k.blocks():
            k.put(Plane(logs, i + 1), r, jnp.log(c[i, r:r + k.n]))
    for r in k.blocks():
        models = k.models_beside(ae, ao, other, r)
        for s, i in enumerate(edge):
            vel, con = models[s]
            k.put(Plane(rims, s), r, jnp.where(k.has[s], vel, v[i, r:r + k.n]))
            k.put(
                Plane(logs, (0, tile + 1)[s]), r,
                jnp.where(k.has[s], jnp.log(con), logs[i + 1, r:r + k.n]),
            )
    for i in range(tile):
        below, above = near(lambda j: Plane(v, j), i, tile, (Plane(rims, 0), Plane(rims, 1)))
        for r in k.blocks():
            vx = (k.get(above, r) - k.get(below, r)) * 0.5
            lx = (logs[i + 2, r:r + k.n] - logs[i, r:r + k.n]) * 0.5
            _, up, down, left, right = k.shifts(Plane(v, i), r, True)
            vy, vz = (down - up) * 0.5, (right - left) * 0.5
            _, up, down, left, right = k.shifts(Plane(logs, i + 1), r, True)
            ly, lz = (down - up) * 0.5, (right - left) * 0.5
            ca = vy * lz - vz * ly
            cb = vz * lx - vx * lz
            cc = vx * ly - vy * lx
            k.put(Plane(pen, i), r, penalty_gain * (ca * ca + cb * cb + cc * cc))


def weigh_kernel(labels, far_labels, mine, other, out):
    _, planes, ny, nz = out.shape
    k = Work(None, ny, nz)
    last = labels.shape[0] - 8
    one, two = (jnp.broadcast_to(ref[last:last + 1], (k.n, nz)) for ref in (labels, far_labels))
    for i in range(planes):
        for r in k.blocks():
            at = slice(i * ny + r, i * ny + r + k.n)
            k.put(Plane(out, 0, i), r, one * mine[at] + two * other[at])
            k.put(Plane(out, 1, i), r, (1.0 - one) * mine[at] + (1.0 - two) * other[at])


def renew(scale, value, gradient, pen):
    return value * jnp.exp(-step_size * jnp.tanh(scale * gradient + pen))


class Sums:
    def __init__(self, part, rest, part_edge, rest_edge):
        self.inner, self.edge = (part, rest), (part_edge, rest_edge)
        self.tile = part.shape[1] + 2

    def get(self, n, i, at):
        edges = (0, self.tile - 1)
        pair, j = (self.edge, edges.index(i)) if i in edges else (self.inner, i - 1)
        return pair[0][n, j, at] + pair[1][n, j, at]


def renew_kernel(scale, w, part, rest, part_edge, rest_edge, pen, v, c, coef, e, o):
    tile, ny, nz = v.shape
    k = Work(w, ny, nz)
    sums = Sums(part, rest, part_edge, rest_edge)
    sound = k.a == 1.0
    for i in range(tile):
        for r in k.blocks():
            at = slice(r, r + k.n)
            new = renew(
                scale,
                jnp.where(sound, v[i, at], c[i, at]),
                jnp.where(sound, sums.get(0, i, at), sums.get(1, i, at)),
                pen[i, at],
            )
            k.put(
                Plane(coef, i), r,
                jnp.where(sound, speed_gain * new**2, diffuse_gain / new),
            )
    k.pack(e, o, [Plane(coef, 0), Plane(coef, 1)], [Plane(coef, tile - 2), Plane(coef, tile - 1)])


def models_kernel(scale, part, rest, part_edge, rest_edge, pen, v, c, out):
    tile, ny, nz = v.shape
    k = Work(None, ny, nz)
    sums = Sums(part, rest, part_edge, rest_edge)
    for n, ref in enumerate((v, c)):
        for i in range(tile):
            for r in k.blocks():
                at = slice(r, r + k.n)
                out[n, i, at] = renew(scale, ref[i, at], sums.get(n, i, at), pen[i, at])


def before_kernel(
    w, coef, old, ends, two, wtwo, three, uthree, winner, halo, beyond, ue, uo, we, wo,
    rim, six, ring, lap, side, wide, prev, last, wthree, four, five,
):
    tile, ny, nz = coef.shape
    k = Work(w, ny, nz)
    edge = (0, tile - 1)
    for r in k.blocks():
        for s, value in enumerate(k.unpack(we, wo, 0, r)):
            k.put(Plane(last, s), r, value)
    for n in range(2):
        far = (((ue, uo, 0), (ue, uo, 1), (ue, uo, 2)), ((ue, uo, 3), (we, wo, 1), (we, wo, 2)))[n]
        for r in k.blocks():
            at = slice(r, r + k.n)
            two_far, three_far, three_end = (k.unpack(*block, r) for block in far)
            for s in range(2):
                wide[(1, tile + 4)[s], at] = three_far[s]
                wide[(0, tile + 5)[s], at] = three_end[s]
                prev[s, at] = two_far[s]

        def second(i):
            return Plane(wtwo, edge.index(i)) if n and i in edge else Plane(two, n, i)

        for s, i in enumerate(edge):
            known = Plane(last, s) if n else Plane(beyond, s, 0)
            earlier = Plane(beyond, s, 1) if n else Plane(halo, s, 1)
            k.step(
                Plane(side, n, s), known, earlier, Plane(halo, s, 0), second(i), Plane(prev, s),
            )
            if n:
                k.step(
                    Plane(wthree, s), second(i), Plane(ends, 1, s), Plane(old, i),
                    *near(second, i, tile, (Plane(last, 0), Plane(last, 1))),
                )
            for r in k.blocks():
                k.put(Plane(wide, (2, tile + 3)[s]), r, side[n, s, r:r + k.n])

        def third_plane(i):
            if i in edge:
                return Plane(wthree if n else uthree, edge.index(i))
            return Plane(winner, i - 1) if n else Plane(three, i)

        for i in range(tile):
            for r in k.blocks():
                k.put(Plane(wide, i + 3), r, k.get(third_plane(i), r))

        for i in range(tile):
            k.step(
                Plane(four, i), Plane(wide, i + 3), second(i), Plane(coef, i),
                Plane(wide, i + 2), Plane(wide, i + 4),
            )
        for s in range(2):
            for m, j in enumerate(((-2, -1), (tile + 1, tile))[s]):
                known = Plane(last, s) if n else Plane(beyond, s, 0)
                earlier = known if m else Plane(prev, s)
                for r in k.blocks():
                    value, total = k.lap(Plane(wide, j + 3), Plane(wide, j + 2), Plane(wide, j + 4), r)
                    k.put(Plane(ring, n, s, m), r, k.ahead(value, k.get(earlier, r)))
                    k.put(Plane(lap, n, s, m), r, total)
        for i in range(tile):
            k.step(
                Plane(five, i), Plane(four, i), third_plane(i), Plane(coef, i),
                *near(lambda j: Plane(four, j), i, tile),
            )
        for i in range(tile):
            k.step(
                Plane(six, n, i), Plane(five, i), Plane(four, i), Plane(coef, i),
                *near(lambda j: Plane(five, j), i, tile),
            )
        for s, i in enumerate(edge):
            for r in k.blocks():
                k.put(Plane(rim, n, s), r, k.get(Plane(four, i), r))


def after_kernel(w, coef, rim, six, ring, lap, side, e, o, out, res, close, away, d, h5, sems):
    _, tile, ny, nz = six.shape
    k = Work(w, ny, nz)
    edge, next_to = (0, tile - 1), (1, tile - 2)
    copies = []

    def send(n, i):
        copies.append(pltpu.make_async_copy(res.at[n, i], out.at[0, n, i], sems.at[n, i]))
        copies[-1].start()

    for n in range(2):
        for i in range(2, tile - 2):
            for r in k.blocks():
                k.put(Plane(res, n, i), r, k.get(Plane(six, n, i), r))
            send(n, i)
        for s, i in enumerate(edge):
            for r in k.blocks():
                at = slice(r, r + k.n)
                outer, inner = (k.unpack(e, o, (m, 1 - m)[s], r)[s] for m in range(2))
                near_plane = ring[n, s, 1, at] + inner * lap[n, s, 1, at]
                close[n, s, at] = near_plane
                away[n, s, at] = (
                    k.ahead(near_plane, side[n, s, at])
                    + inner * (ring[n, s, 0, at] + outer * lap[n, s, 0, at] + rim[n, s, at])
                )
                h5[n, s, at] = inner
                delta = coef[i, at] * near_plane
                d[n, s, at] = delta
                j = next_to[s]
                res[n, j, at] = six[n, j, at] + coef[j, at] * delta
            send(n, next_to[s])
        for s, i in enumerate(edge):
            for r in k.blocks():
                at = slice(r, r + k.n)
                _, total = k.flat(Plane(close, n, s), r)
                fifth = away[n, s, at] + h5[n, s, at] * total
                delta, total = k.flat(Plane(d, n, s), r)
                res[n, i, at] = (
                    six[n, i, at] + (1.0 + k.a) * delta + coef[i, at] * (total + fifth)
                )
            send(n, i)
    for copy in copies:
        copy.wait()


def swap_pairs(even_block, odd_block):
    count, groups = lax.axis_size("space"), lax.axis_size("src")

    def swap(block, partner):
        pairs = []
        for g in range(groups):
            for i in range(count):
                j = partner(i)
                to = g * count + j if 0 <= j < count else (g ^ 1) * count + i
                pairs.append((g * count + i, to))
        return lax.ppermute(block, ("src", "space"), pairs)

    odd_block = swap(odd_block, lambda i: ((i + 1) ^ 1) - 1)
    even_block = swap(even_block, lambda i: i ^ 1)
    return even_block, odd_block


def across(block, mask):
    count = lax.axis_size("src")
    return lax.ppermute(block, "src", [(i, i ^ mask) for i in range(count)])


def block_step(fields, velocity, conductivity, labels):
    tile, ny, nz = velocity.shape
    groups = lax.axis_size("src")
    assert tile >= 4 and labels.shape[0] == 1 and groups >= 4 and groups & (groups - 1) == 0
    scale = 1.0 / (20.0 * math.sqrt(groups))

    def planes(*lead):
        return (*lead, ny, nz)

    ae, ao = call(
        fetch_kernel,
        [planes(2)] * 2,
        tuple(pltpu.with_memory_space_constraint(x, pltpu.HBM) for x in (fields, velocity, conductivity)),
        [planes(3, 2)],
        [pl.BlockSpec(memory_space=pltpu.HBM)] * 3,
        [pltpu.SemaphoreType.DMA((3, 2))],
    )
    ae, ao = swap_pairs(ae, ao)
    de, do, coef, w = call(
        lead_kernel,
        [planes(2)] * 2 + [planes(tile), (8, nz)],
        (labels, fields, velocity, conductivity),
        [planes(2)],
        [pl.BlockSpec(memory_space=pltpu.SMEM)] + [VMEM] * 3,
    )
    de, do = swap_pairs(de, do)
    be, bo, one, acc = call(
        isolated_kernel,
        [planes(2)] * 2 + [planes(2, tile), planes(tile)],
        (w, fields, coef),
        [planes(2)],
    )
    be, bo = swap_pairs(be, bo)
    (other,) = call(pick_kernel, [planes(2)], (ae, ao))
    other = across(other, 1)

    acc1, rim, ends, two, three, halo = call(
        inner_kernel,
        [((tile - 2) * ny + 8, nz), planes(2), planes(2, 2), planes(2, tile), planes(tile), planes(2, 2)],
        (w, fields, coef, one, acc, ae, ao, de, do, other),
        [planes(2)],
    )
    masks = [1 << k for k in reversed(range(groups.bit_length() - 1))]
    far1 = across(acc1, masks[0])
    ue, uo = call(early_u_kernel, [planes(4)] * 2, (two, three))
    ue, uo = swap_pairs(ue, uo)
    acc2, wtwo, uthree, beyond = call(
        outer_kernel,
        [(2 * ny, nz), planes(2), planes(2), planes(2, 2)],
        (w, fields, coef, one, ends, two, halo, rim, be, bo),
        [planes(2)],
    )
    far2 = across(acc2, masks[0])
    we, wo, winner = call(
        early_w_kernel, [planes(3), planes(3), planes(tile - 2)], (w, coef, one, two, wtwo)
    )
    we, wo = swap_pairs(we, wo)
    (pen,) = call(
        penalty_kernel,
        [planes(tile)],
        (velocity, conductivity, ae, ao, other),
        [planes(tile + 2), planes(2)],
    )

    sums = []
    for mine, far in ((acc1, far1), (acc2, far2)):
        rows = mine.shape[0] // ny
        (part,) = call(weigh_kernel, [planes(2, rows)], (acc1, far1, mine, far))
        for mask in masks[1:-1]:
            part = part + across(part, mask)
        sums += [part, across(part, masks[-1])]
    coef_next, e, o = call(
        lambda *refs: renew_kernel(scale, *refs),
        [planes(tile), planes(2), planes(2)],
        (w, *sums, pen, velocity, conductivity),
    )
    e, o = swap_pairs(e, o)
    (models,) = call(
        lambda *refs: models_kernel(scale, *refs),
        [planes(2, tile)], (*sums, pen, velocity, conductivity),
    )
    rim, six, ring, lap, side = call(
        before_kernel,
        [planes(2, 2), planes(2, tile), planes(2, 2, 2), planes(2, 2, 2), planes(2, 2)],
        (w, coef_next, coef, ends, two, wtwo, three, uthree, winner, halo, beyond, ue, uo, we, wo),
        [planes(tile + 6), planes(2), planes(2), planes(2), planes(tile), planes(tile)],
    )
    (final,) = call(
        after_kernel,
        [planes(1, 2, tile)],
        (w, coef_next, rim, six, ring, lap, side, e, o),
        [planes(2, tile), planes(2, 2), planes(2, 2), planes(2, 2), planes(2, 2)],
        None,
        [pltpu.SemaphoreType.DMA((2, tile))],
        pl.BlockSpec(memory_space=pltpu.HBM),
    )
    return final, models


def solution(mesh):
    in_specs = (
        P(("parts", "src"), None, "space", None, None),
        P(("parts", "space"), None, None),
        P(("parts", "space"), None, None),
        P(("parts", "src")),
    )
    out_specs = (
        P(("parts", "src"), None, "space", None, None),
        P(None, ("parts", "space"), None, None),
    )
    return jax.shard_map(
        block_step, mesh=mesh, in_specs=in_specs, out_specs=out_specs, check_vma=False
    )
```

```python
import math

import jax
import jax.numpy as jnp
from jax import lax
from jax.experimental import pallas as pl
from jax.experimental.pallas import tpu as pltpu
from jax.sharding import PartitionSpec as P


speed_gain = 0.25
diffuse_gain = 0.15
step_size = 0.1
penalty_gain = 50.0

VMEM = pl.BlockSpec(memory_space=pltpu.VMEM)
F32 = jnp.float32


def call(kernel, outs, args, scratch=(), specs=None, extra=(), out_spec=VMEM):
    size = sum(math.prod(o) for o in outs) + sum(a.size for a in args)
    return pl.pallas_call(
        kernel,
        out_shape=tuple(jax.ShapeDtypeStruct(o, F32) for o in outs),
        in_specs=specs or [VMEM for _ in args],
        out_specs=tuple(out_spec for _ in outs),
        scratch_shapes=[pltpu.VMEM(s, F32) for s in scratch] + list(extra),
        compiler_params=pltpu.CompilerParams(vmem_limit_bytes=16 << 20),
        cost_estimate=pl.CostEstimate(flops=20 * size, bytes_accessed=4 * size, transcendentals=0),
    )(*args)


class Plane:
    def __init__(self, ref, *at, base=0):
        self.ref, self.at, self.base = ref, at, base

    def _rows(self, r, n):
        return (*self.at, slice(self.base + r, self.base + r + n))

    def get(self, r, n):
        return self.ref[self._rows(r, n)]

    def put(self, r, n, value):
        self.ref[self._rows(r, n)] = value


class Work:
    def __init__(self, weight_ref, ny, nz):
        self.ny, self.n = ny, 32 if ny % 32 == 0 else ny
        shape = (self.n, nz)
        row = lax.broadcasted_iota(jnp.int32, shape, 0)
        col = lax.broadcasted_iota(jnp.int32, shape, 1)
        self.top, self.bottom = row == 0, row == self.n - 1
        self.left, self.right = col == 0, col == nz - 1
        self.nz = nz
        if weight_ref is not None:
            self.a = jnp.broadcast_to(weight_ref[0:1], shape)
        here = lax.axis_index("space")
        self.even = here % 2 == 0
        self.has = (here > 0, here < lax.axis_size("space") - 1)
        self.first_core = lax.axis_index("src") % 2 == 0

    def blocks(self):
        return range(0, self.ny, self.n)

    def get(self, plane, r):
        return plane.get(r, self.n)

    def put(self, plane, r, value):
        plane.put(r, self.n, value)

    def shifts(self, plane, r, edge):
        n, v = self.n, plane.get(r, self.n)

        def fill(test, moved):
            return jnp.where(test, v if edge else 0.0, moved)

        up = plane.get(r - 1, n) if r > 0 else fill(self.top, pltpu.roll(v, 1, 0))
        last = r + n == self.ny
        down = fill(self.bottom, pltpu.roll(v, n - 1, 0)) if last else plane.get(r + 1, n)
        left = fill(self.left, pltpu.roll(v, 1, 1))
        right = fill(self.right, pltpu.roll(v, self.nz - 1, 1))
        return v, up, down, left, right

    def flat(self, plane, r):
        v, up, down, left, right = self.shifts(plane, r, False)
        return v, ((up + down) + (left + right)) - 6.0 * v

    def lap(self, plane, below, above, r):
        v, total = self.flat(plane, r)
        for other in (below, above):
            if other is not None:
                total = total + self.get(other, r)
        return v, total

    def ahead(self, v, before):
        return (1.0 + self.a) * v - self.a * before

    def step(self, out, now, before, coef, below, above, each=None):
        for r in self.blocks():
            v, total = self.lap(now, below, above, r)
            value = self.ahead(v, self.get(before, r)) + self.get(coef, r) * total
            if out is not None:
                self.put(out, r, value)
            if each is not None:
                each(r, v, total, value)

    def coefficient(self, v, c):
        return self.a * speed_gain * v**2 + (1.0 - self.a) * diffuse_gain / c

    def models_beside(self, even_ref, odd_ref, other, r):
        mine = self.unpack(even_ref, odd_ref, 0, r)
        theirs = self.unpack(other.at[0:1], other.at[1:2], 0, r)
        out = []
        for s in range(2):
            vel = jnp.where(self.first_core, mine[s], theirs[s])
            con = jnp.where(self.first_core, theirs[s], mine[s])
            out.append((jnp.where(self.has[s], vel, 1.0), jnp.where(self.has[s], con, 1.0)))
        return out

    def pack(self, even_ref, odd_ref, lows, highs):
        for k, (low, high) in enumerate(zip(lows, highs)):
            for r in self.blocks():
                lo, hi = self.get(low, r), self.get(high, r)
                self.put(Plane(even_ref, k), r, jnp.where(self.even, hi, lo))
                self.put(Plane(odd_ref, k), r, jnp.where(self.even, lo, hi))

    def unpack(self, even_ref, odd_ref, k, r):
        e, o = self.get(Plane(even_ref, k), r), self.get(Plane(odd_ref, k), r)
        low, high = jnp.where(self.even, o, e), jnp.where(self.even, e, o)
        return jnp.where(self.has[0], low, 0.0), jnp.where(self.has[1], high, 0.0)


def near(make, i, tile, ends=(None, None)):
    return (make(i - 1) if i > 0 else ends[0]), (make(i + 1) if i < tile - 1 else ends[1])


def fetch_kernel(f_in, v_in, c_in, even, odd, sems):
    tile, ny, nz = v_in.shape
    k = Work(None, ny, nz)
    high = (tile - 1) * k.even.astype(jnp.int32)
    places = ((even, high), (odd, tile - 1 - high))

    def model(src):
        for n, (out, at) in enumerate(places):
            pltpu.make_async_copy(src.at[at], out.at[0], sems.at[0, n]).start()

    pl.when(k.first_core)(lambda: model(v_in))
    pl.when(jnp.logical_not(k.first_core))(lambda: model(c_in))
    for n, (out, at) in enumerate(places):
        pltpu.make_async_copy(f_in.at[0, 0, at], out.at[1], sems.at[1, n]).start()
    for n, (out, at) in enumerate(places):
        pltpu.make_async_copy(v_in.at[at], out.at[0], sems.at[0, n]).wait()
        pltpu.make_async_copy(f_in.at[0, 0, at], out.at[1], sems.at[1, n]).wait()


def lead_kernel(label, f, v, c, even, odd, coef, w, one):
    tile, ny, nz = v.shape
    w[...] = jnp.full(w.shape, label[0].astype(F32), F32)
    k = Work(w, ny, nz)
    edge = (0, tile - 1)
    for i in range(tile):
        for r in k.blocks():
            k.put(Plane(coef, i), r, k.coefficient(v[i, r:r + k.n], c[i, r:r + k.n]))
    for s, i in enumerate(edge):
        k.step(
            Plane(one, s), Plane(f, 0, 0, i), Plane(f, 0, 1, i), Plane(coef, i),
            *near(lambda j: Plane(f, 0, 0, j), i, tile),
        )
    k.pack(even, odd, *([Plane(f, 0, 2, i), Plane(one, s)] for s, i in enumerate(edge)))


def isolated_kernel(w, f, coef, be, bo, one, acc, two):
    tile, ny, nz = coef.shape
    k = Work(w, ny, nz)
    edge = (0, tile - 1)
    for n in range(2):
        for i in range(tile):

            def each(r, value, total, out, i=i):
                k.put(Plane(acc, i), r, f[0, 2, i, r:r + k.n] * total)

            k.step(
                Plane(one, n, i), Plane(f, 0, 2 * n, i), Plane(f, 0, 2 * n + 1, i), Plane(coef, i),
                *near(lambda j: Plane(f, 0, 2 * n, j), i, tile), each if n == 0 else None,
            )
    for s, i in enumerate(edge):
        k.step(
            Plane(two, s), Plane(one, 0, i), Plane(f, 0, 0, i), Plane(coef, i),
            *near(lambda j: Plane(one, 0, j), i, tile),
        )
    k.pack(be, bo, *([Plane(two, s), Plane(one, 1, i)] for s, i in enumerate(edge)))


def inner_kernel(
    w, f, coef, one, acc, ae, ao, de, do, other, acc1, rim, ends, two, three, halo, zero,
):
    tile, ny, nz = coef.shape
    k = Work(w, ny, nz)
    edge = (0, tile - 1)
    for r in k.blocks():
        models = k.models_beside(ae, ao, other, r)
        parts = [k.unpack(ae, ao, 1, r)] + [k.unpack(de, do, m, r) for m in range(2)]
        for s, i in enumerate(edge):
            h = [jnp.where(k.has[s], k.coefficient(*models[s]), 0.0)] + [p[s] for p in parts]
            cf, w0, u0 = coef[i, r:r + k.n], f[0, 2, i, r:r + k.n], f[0, 0, i, r:r + k.n]
            k.put(Plane(halo, s, 0), r, h[0])
            k.put(Plane(halo, s, 1), r, h[3] + h[0] * u0)
            k.put(Plane(ends, 0, s), r, one[0, i, r:r + k.n] + cf * h[1])
            k.put(Plane(ends, 1, s), r, one[1, i, r:r + k.n] + cf * h[2])
            k.put(Plane(zero, s), r, acc[i, r:r + k.n] + w0 * h[1])

    def first(n, i):
        return Plane(ends, n, edge.index(i)) if i in edge else Plane(one, n, i)

    def inside(i):
        return Plane(acc1, base=(i - 1) * ny)

    outside = (Plane(halo, 0, 1), Plane(halo, 1, 1))
    for i in range(tile):

        def each(r, value, total, out, i=i):
            term = k.get(first(1, i), r) * total
            if i in edge:
                s = edge.index(i)
                k.put(Plane(rim, s), r, zero[s, r:r + k.n] + term)
            else:
                k.put(inside(i), r, acc[i, r:r + k.n] + term)

        k.step(
            Plane(two, 0, i), first(0, i), Plane(f, 0, 0, i), Plane(coef, i),
            *near(lambda j: first(0, j), i, tile, outside), each,
        )
    for i in range(1, tile - 1):
        k.step(
            Plane(two, 1, i), first(1, i), Plane(f, 0, 2, i), Plane(coef, i),
            *near(lambda j: first(1, j), i, tile),
        )
    for i in range(1, tile - 1):

        def each(r, value, total, out, i=i):
            k.put(inside(i), r, k.get(inside(i), r) + two[1, i, r:r + k.n] * total)

        k.step(
            Plane(three, i), Plane(two, 0, i), first(0, i), Plane(coef, i),
            *near(lambda j: Plane(two, 0, j), i, tile), each,
        )
    rows = (tile - 2) * ny
    acc1[rows:] = jnp.broadcast_to(w[0:1], (acc1.shape[0] - rows, nz))
    for i in edge:
        for r in k.blocks():
            k.put(Plane(two, 1, i), r, jnp.zeros((k.n, nz), F32))


def outer_kernel(w, f, coef, one, ends, two, halo, rim, be, bo, acc2, wtwo, uthree, beyond, d):
    tile, ny, nz = coef.shape
    k = Work(w, ny, nz)
    edge = (0, tile - 1)
    for s, i in enumerate(edge):
        for r in k.blocks():
            k.put(Plane(d, s), r, halo[s, 0, r:r + k.n] * f[0, 0, i, r:r + k.n])
    for r in k.blocks():
        u2, w1 = k.unpack(be, bo, 0, r), k.unpack(be, bo, 1, r)
        for s, i in enumerate(edge):
            h = halo[s, 0, r:r + k.n]
            dv, total = k.flat(Plane(d, s), r)
            total = total + ends[0, s, r:r + k.n]
            k.put(Plane(beyond, s, 0), r, u2[s] + (1.0 + k.a) * dv + h * total)
            k.put(Plane(beyond, s, 1), r, w1[s] + h * f[0, 2, i, r:r + k.n])

    def first(n, i):
        return Plane(ends, n, edge.index(i)) if i in edge else Plane(one, n, i)

    for s, i in enumerate(edge):
        k.step(
            Plane(wtwo, s), first(1, i), Plane(f, 0, 2, i), Plane(coef, i),
            *near(lambda j: first(1, j), i, tile, (Plane(beyond, 0, 1), Plane(beyond, 1, 1))),
        )

        def each(r, value, total, out, s=s):
            k.put(
                Plane(acc2, base=s * ny), r,
                rim[s, r:r + k.n] + wtwo[s, r:r + k.n] * total,
            )

        k.step(
            Plane(uthree, s), Plane(two, 0, i), first(0, i), Plane(coef, i),
            *near(lambda j: Plane(two, 0, j), i, tile, (Plane(beyond, 0, 0), Plane(beyond, 1, 0))),
            each,
        )


def early_u_kernel(two, three, pe, po):
    _, tile, ny, nz = two.shape
    k = Work(None, ny, nz)

    def planes(i, j):
        return [Plane(two, 0, i), Plane(three, i), Plane(three, j), Plane(two, 1, i)]

    k.pack(pe, po, planes(1, 2), planes(tile - 2, tile - 3))


def early_w_kernel(w, coef, one, two, wtwo, pe, po, winner):
    tile, ny, nz = coef.shape
    k = Work(w, ny, nz)
    edge = (0, tile - 1)

    def second(i):
        return Plane(wtwo, edge.index(i)) if i in edge else Plane(two, 1, i)

    for i in range(1, tile - 1):
        k.step(
            Plane(winner, i - 1), second(i), Plane(one, 1, i), Plane(coef, i),
            *near(second, i, tile),
        )

    def planes(s, i, j):
        return [Plane(wtwo, s), Plane(winner, i - 1), Plane(winner, j - 1)]

    k.pack(pe, po, planes(0, 1, 2), planes(1, tile - 2, tile - 3))


def pick_kernel(even, odd, out):
    out[0], out[1] = even[0], odd[0]


def penalty_kernel(v, c, ae, ao, other, pen, logs, rims):
    tile, ny, nz = v.shape
    k = Work(None, ny, nz)
    edge = (0, tile - 1)
    for i in range(tile):
        for r in k.blocks():
            k.put(Plane(logs, i + 1), r, jnp.log(c[i, r:r + k.n]))
    for r in k.blocks():
        models = k.models_beside(ae, ao, other, r)
        for s, i in enumerate(edge):
            vel, con = models[s]
            k.put(Plane(rims, s), r, jnp.where(k.has[s], vel, v[i, r:r + k.n]))
            k.put(
                Plane(logs, (0, tile + 1)[s]), r,
                jnp.where(k.has[s], jnp.log(con), logs[i + 1, r:r + k.n]),
            )
    for i in range(tile):
        below, above = near(lambda j: Plane(v, j), i, tile, (Plane(rims, 0), Plane(rims, 1)))
        for r in k.blocks():
            vx = (k.get(above, r) - k.get(below, r)) * 0.5
            lx = (logs[i + 2, r:r + k.n] - logs[i, r:r + k.n]) * 0.5
            _, up, down, left, right = k.shifts(Plane(v, i), r, True)
            vy, vz = (down - up) * 0.5, (right - left) * 0.5
            _, up, down, left, right = k.shifts(Plane(logs, i + 1), r, True)
            ly, lz = (down - up) * 0.5, (right - left) * 0.5
            ca = vy * lz - vz * ly
            cb = vz * lx - vx * lz
            cc = vx * ly - vy * lx
            k.put(Plane(pen, i), r, penalty_gain * (ca * ca + cb * cb + cc * cc))


def weigh_kernel(labels, far_labels, mine, other, out):
    _, planes, ny, nz = out.shape
    k = Work(None, ny, nz)
    last = labels.shape[0] - 8
    one, two = (jnp.broadcast_to(ref[last:last + 1], (k.n, nz)) for ref in (labels, far_labels))
    for i in range(planes):
        for r in k.blocks():
            at = slice(i * ny + r, i * ny + r + k.n)
            k.put(Plane(out, 0, i), r, one * mine[at] + two * other[at])
            k.put(Plane(out, 1, i), r, (1.0 - one) * mine[at] + (1.0 - two) * other[at])


def renew(scale, value, gradient, pen):
    return value * jnp.exp(-step_size * jnp.tanh(scale * gradient + pen))


class Sums:
    def __init__(self, part, rest, part_edge, rest_edge):
        self.inner, self.edge = (part, rest), (part_edge, rest_edge)
        self.tile = part.shape[1] + 2

    def get(self, n, i, at):
        edges = (0, self.tile - 1)
        pair, j = (self.edge, edges.index(i)) if i in edges else (self.inner, i - 1)
        return pair[0][n, j, at] + pair[1][n, j, at]


def renew_kernel(scale, w, part, rest, part_edge, rest_edge, pen, v, c, coef, e, o):
    tile, ny, nz = v.shape
    k = Work(w, ny, nz)
    sums = Sums(part, rest, part_edge, rest_edge)
    sound = k.a == 1.0
    for i in range(tile):
        for r in k.blocks():
            at = slice(r, r + k.n)
            new = renew(
                scale,
                jnp.where(sound, v[i, at], c[i, at]),
                jnp.where(sound, sums.get(0, i, at), sums.get(1, i, at)),
                pen[i, at],
            )
            k.put(
                Plane(coef, i), r,
                jnp.where(sound, speed_gain * new**2, diffuse_gain / new),
            )
    k.pack(e, o, [Plane(coef, 0), Plane(coef, 1)], [Plane(coef, tile - 2), Plane(coef, tile - 1)])


def models_kernel(scale, part, rest, part_edge, rest_edge, pen, v, c, out):
    tile, ny, nz = v.shape
    k = Work(None, ny, nz)
    sums = Sums(part, rest, part_edge, rest_edge)
    for n, ref in enumerate((v, c)):
        for i in range(tile):
            for r in k.blocks():
                at = slice(r, r + k.n)
                out[n, i, at] = renew(scale, ref[i, at], sums.get(n, i, at), pen[i, at])


def before_kernel(
    w, coef, old, ends, two, wtwo, three, uthree, winner, halo, beyond, ue, uo, we, wo,
    rim, six, ring, lap, side, wide, prev, last, wthree, four, five,
):
    tile, ny, nz = coef.shape
    k = Work(w, ny, nz)
    edge = (0, tile - 1)
    for r in k.blocks():
        for s, value in enumerate(k.unpack(we, wo, 0, r)):
            k.put(Plane(last, s), r, value)
    for n in range(2):
        far = (((ue, uo, 0), (ue, uo, 1), (ue, uo, 2)), ((ue, uo, 3), (we, wo, 1), (we, wo, 2)))[n]
        for r in k.blocks():
            at = slice(r, r + k.n)
            two_far, three_far, three_end = (k.unpack(*block, r) for block in far)
            for s in range(2):
                wide[(1, tile + 4)[s], at] = three_far[s]
                wide[(0, tile + 5)[s], at] = three_end[s]
                prev[s, at] = two_far[s]

        def second(i):
            return Plane(wtwo, edge.index(i)) if n and i in edge else Plane(two, n, i)

        for s, i in enumerate(edge):
            known = Plane(last, s) if n else Plane(beyond, s, 0)
            earlier = Plane(beyond, s, 1) if n else Plane(halo, s, 1)
            k.step(
                Plane(side, n, s), known, earlier, Plane(halo, s, 0), second(i), Plane(prev, s),
            )
            if n:
                k.step(
                    Plane(wthree, s), second(i), Plane(ends, 1, s), Plane(old, i),
                    *near(second, i, tile, (Plane(last, 0), Plane(last, 1))),
                )
            for r in k.blocks():
                k.put(Plane(wide, (2, tile + 3)[s]), r, side[n, s, r:r + k.n])

        def third_plane(i):
            if i in edge:
                return Plane(wthree if n else uthree, edge.index(i))
            return Plane(winner, i - 1) if n else Plane(three, i)

        for i in range(tile):
            for r in k.blocks():
                k.put(Plane(wide, i + 3), r, k.get(third_plane(i), r))

        for i in range(tile):
            k.step(
                Plane(four, i), Plane(wide, i + 3), second(i), Plane(coef, i),
                Plane(wide, i + 2), Plane(wide, i + 4),
            )
        for s in range(2):
            for m, j in enumerate(((-2, -1), (tile + 1, tile))[s]):
                known = Plane(last, s) if n else Plane(beyond, s, 0)
                earlier = known if m else Plane(prev, s)
                for r in k.blocks():
                    value, total = k.lap(Plane(wide, j + 3), Plane(wide, j + 2), Plane(wide, j + 4), r)
                    k.put(Plane(ring, n, s, m), r, k.ahead(value, k.get(earlier, r)))
                    k.put(Plane(lap, n, s, m), r, total)
        for i in range(tile):
            k.step(
                Plane(five, i), Plane(four, i), third_plane(i), Plane(coef, i),
                *near(lambda j: Plane(four, j), i, tile),
            )
        for i in range(tile):
            k.step(
                Plane(six, n, i), Plane(five, i), Plane(four, i), Plane(coef, i),
                *near(lambda j: Plane(five, j), i, tile),
            )
        for s, i in enumerate(edge):
            for r in k.blocks():
                k.put(Plane(rim, n, s), r, k.get(Plane(four, i), r))


def after_kernel(w, coef, rim, six, ring, lap, side, e, o, out, res, close, away, d, h5, sems):
    _, tile, ny, nz = six.shape
    k = Work(w, ny, nz)
    edge, next_to = (0, tile - 1), (1, tile - 2)
    copies = []

    def send(n, i):
        copies.append(pltpu.make_async_copy(res.at[n, i], out.at[0, n, i], sems.at[n, i]))
        copies[-1].start()

    for n in range(2):
        for i in range(2, tile - 2):
            for r in k.blocks():
                k.put(Plane(res, n, i), r, k.get(Plane(six, n, i), r))
            send(n, i)
    for s, i in enumerate(edge):
        j = next_to[s]
        for r in k.blocks():
            at = slice(r, r + k.n)
            outer, inner = (k.unpack(e, o, (m, 1 - m)[s], r)[s] for m in range(2))
            h5[s, at] = inner
            for n in range(2):
                near_plane = ring[n, s, 1, at] + inner * lap[n, s, 1, at]
                close[n, s, at] = near_plane
                away[n, s, at] = (
                    k.ahead(near_plane, side[n, s, at])
                    + inner * (ring[n, s, 0, at] + outer * lap[n, s, 0, at] + rim[n, s, at])
                )
                delta = coef[i, at] * near_plane
                d[n, s, at] = delta
                res[n, j, at] = six[n, j, at] + coef[j, at] * delta
        for n in range(2):
            send(n, j)
        for n in range(2):
            for r in k.blocks():
                at = slice(r, r + k.n)
                _, total = k.flat(Plane(close, n, s), r)
                fifth = away[n, s, at] + h5[s, at] * total
                delta, total = k.flat(Plane(d, n, s), r)
                res[n, i, at] = (
                    six[n, i, at] + (1.0 + k.a) * delta + coef[i, at] * (total + fifth)
                )
            send(n, i)
    for copy in copies:
        copy.wait()


def swap_pairs(even_block, odd_block):
    count, groups = lax.axis_size("space"), lax.axis_size("src")

    def swap(block, partner):
        pairs = []
        for g in range(groups):
            for i in range(count):
                j = partner(i)
                to = g * count + j if 0 <= j < count else (g ^ 1) * count + i
                pairs.append((g * count + i, to))
        return lax.ppermute(block, ("src", "space"), pairs)

    odd_block = swap(odd_block, lambda i: ((i + 1) ^ 1) - 1)
    even_block = swap(even_block, lambda i: i ^ 1)
    return even_block, odd_block


def across(block, mask):
    count = lax.axis_size("src")
    return lax.ppermute(block, "src", [(i, i ^ mask) for i in range(count)])


def block_step(fields, velocity, conductivity, labels):
    tile, ny, nz = velocity.shape
    groups = lax.axis_size("src")
    assert tile >= 4 and labels.shape[0] == 1 and groups >= 4 and groups & (groups - 1) == 0
    scale = 1.0 / (20.0 * math.sqrt(groups))

    def planes(*lead):
        return (*lead, ny, nz)

    ae, ao = call(
        fetch_kernel,
        [planes(2)] * 2,
        tuple(pltpu.with_memory_space_constraint(x, pltpu.HBM) for x in (fields, velocity, conductivity)),
        (),
        [pl.BlockSpec(memory_space=pltpu.HBM)] * 3,
        [pltpu.SemaphoreType.DMA((2, 2))],
    )
    ae, ao = swap_pairs(ae, ao)
    de, do, coef, w = call(
        lead_kernel,
        [planes(2)] * 2 + [planes(tile), (8, nz)],
        (labels, fields, velocity, conductivity),
        [planes(2)],
        [pl.BlockSpec(memory_space=pltpu.SMEM)] + [VMEM] * 3,
    )
    de, do = swap_pairs(de, do)
    be, bo, one, acc = call(
        isolated_kernel,
        [planes(2)] * 2 + [planes(2, tile), planes(tile)],
        (w, fields, coef),
        [planes(2)],
    )
    be, bo = swap_pairs(be, bo)
    (other,) = call(pick_kernel, [planes(2)], (ae, ao))
    other = across(other, 1)

    acc1, rim, ends, two, three, halo = call(
        inner_kernel,
        [((tile - 2) * ny + 8, nz), planes(2), planes(2, 2), planes(2, tile), planes(tile), planes(2, 2)],
        (w, fields, coef, one, acc, ae, ao, de, do, other),
        [planes(2)],
    )
    masks = [1 << k for k in reversed(range(groups.bit_length() - 1))]
    far1 = across(acc1, masks[0])
    ue, uo = call(early_u_kernel, [planes(4)] * 2, (two, three))
    ue, uo = swap_pairs(ue, uo)
    acc2, wtwo, uthree, beyond = call(
        outer_kernel,
        [(2 * ny, nz), planes(2), planes(2), planes(2, 2)],
        (w, fields, coef, one, ends, two, halo, rim, be, bo),
        [planes(2)],
    )
    far2 = across(acc2, masks[0])
    we, wo, winner = call(
        early_w_kernel, [planes(3), planes(3), planes(tile - 2)], (w, coef, one, two, wtwo)
    )
    we, wo = swap_pairs(we, wo)
    (pen,) = call(
        penalty_kernel,
        [planes(tile)],
        (velocity, conductivity, ae, ao, other),
        [planes(tile + 2), planes(2)],
    )

    sums = []
    for mine, far in ((acc1, far1), (acc2, far2)):
        rows = mine.shape[0] // ny
        (part,) = call(weigh_kernel, [planes(2, rows)], (acc1, far1, mine, far))
        for mask in masks[1:-1]:
            part = part + across(part, mask)
        sums += [part, across(part, masks[-1])]
    coef_next, e, o = call(
        lambda *refs: renew_kernel(scale, *refs),
        [planes(tile), planes(2), planes(2)],
        (w, *sums, pen, velocity, conductivity),
    )
    e, o = swap_pairs(e, o)
    (models,) = call(
        lambda *refs: models_kernel(scale, *refs),
        [planes(2, tile)], (*sums, pen, velocity, conductivity),
    )
    rim, six, ring, lap, side = call(
        before_kernel,
        [planes(2, 2), planes(2, tile), planes(2, 2, 2), planes(2, 2, 2), planes(2, 2)],
        (w, coef_next, coef, ends, two, wtwo, three, uthree, winner, halo, beyond, ue, uo, we, wo),
        [planes(tile + 6), planes(2), planes(2), planes(2), planes(tile), planes(tile)],
    )
    (final,) = call(
        after_kernel,
        [planes(1, 2, tile)],
        (w, coef_next, rim, six, ring, lap, side, e, o),
        [planes(2, tile), planes(2, 2), planes(2, 2), planes(2, 2), planes(2)],
        None,
        [pltpu.SemaphoreType.DMA((2, tile))],
        pl.BlockSpec(memory_space=pltpu.HBM),
    )
    return final, models


def solution(mesh):
    in_specs = (
        P(("parts", "src"), None, "space", None, None),
        P(("parts", "space"), None, None),
        P(("parts", "space"), None, None),
        P(("parts", "src")),
    )
    out_specs = (
        P(("parts", "src"), None, "space", None, None),
        P(None, ("parts", "space"), None, None),
    )
    return jax.shard_map(
        block_step, mesh=mesh, in_specs=in_specs, out_specs=out_specs, check_vma=False
    )
```
